256 devices in a mesh: pp: 2 (over x_hi), dp: 8 (over y, core), cp: 16 (over z, x_lo).
Axes of the slice: x: 4 (x_hi: 2, x_lo: 2; x = x_hi * 2 + x_lo), y: 4, z: 8, core: 2. Of those that a mesh axis runs over, the one named last changes fastest.
Arguments:
- tokens: bfloat16 [2, 2048, 3584], P('pp', 'cp'), may hold values from -6 to 6
- out_grad: bfloat16 [2, 2048, 3584], P('pp', 'cp'), may hold values from -6 to 6
- probs: bfloat16 [2, 2048, 8], P('pp', 'cp'), may hold values from 0.019897461 to 0.29882812
- expert_ids: int32 [2, 2048, 8], P('pp', 'cp'), may hold values from 0 to 15, all different within a row; in each aligned block of 128 rows (0 to 127, 128 to 255, ..., all dimensions but the last counted through in order) at most 80 rows name the same one
- w_gate: bfloat16 [2, 16, 1280, 3584], P('pp', 'cp', 'dp'), may hold values from -0.09375 to 0.09375
- w_up: bfloat16 [2, 16, 1280, 3584], P('pp', 'cp', 'dp'), may hold values from -0.09375 to 0.09375
- w_down: bfloat16 [2, 16, 1280, 3584], P('pp', 'cp', 'dp'), may hold values from -0.15625 to 0.15625
Outputs:
- passed_grad: bfloat16 [2, 2048, 3584], P('pp', 'cp', 'dp')
- prob_grad: float32 [2, 2048, 8], P('pp', 'cp')
- gate_grad: bfloat16 [2, 16, 1280, 3584], P('pp', 'cp', 'dp')
- up_grad: bfloat16 [2, 16, 1280, 3584], P('pp', 'cp', 'dp')
- down_grad: bfloat16 [2, 16, 1280, 3584], P('pp', 'cp', 'dp')
The draws below stay inside these ranges and needn't reach their ends.
Inputs may be any that keep to these rules, and one draw needn't show every extreme that they name: `expert_ids`: in each aligned block of 128 tokens of a section, a token names 8 different experts, and no expert is named by more than 80 tokens of the block; some expert is named by exactly 80 tokens of some block.
All inputs are finite; a program needn't handle non-finite values.
Results may differ from the reference program's by a relative error of at most 0.012.
Values may be sent and summed in bfloat16 or wider, within the bound.
A program may use at most 128 MiB of HBM per device.

```python
import math
import jax
import jax.numpy as jnp
import numpy as np
from jax import lax

D = 3584
FF = 1280
TOK_DEV = 128
SECTIONS = 2
EXPERTS = 16
TOPK = 8
CAP = 80
TOKENS = 2048
N_DP = 8
N_CP = 16


def levels(own_key, shape, shards, low, largest):
    loudness = 1.0
    for axis_at, blocks in shards:
        steps = jax.random.uniform(jax.random.fold_in(jax.random.fold_in(own_key, 6), axis_at), (blocks,), jnp.float32, low / len(shards), largest / len(shards))
        loudness = loudness * jnp.repeat(jnp.exp(steps), shape[axis_at] // blocks).reshape((-1,) + (1,) * (len(shape) - 1 - axis_at))
    return loudness


def routed_block(stream_key, own, number, rows, number_of, top, bound, skew):
    sequence = jax.random.permutation(stream_key, number_of)
    packed, usual = shares(number_of, rows * top, bound, skew, True), shares(number_of, rows * top, bound, skew, False)
    places = jnp.arange(number_of)

    def named(tallies, offset_by):
        used = int((tallies > 0).sum())
        fixed = max(1, used // 4)
        moved = fixed + (places - fixed + offset_by * (used - fixed)) % max(1, number_of - fixed)
        return jnp.zeros((number_of,), jnp.int32).at[sequence[jnp.where(places < fixed, places, moved)]].set(jnp.asarray(tallies, jnp.int32))

    tallies = jnp.where(number % 4 == 0, named(packed, number // 4), named(usual, number - number // 4 - 1))
    mixed = jax.random.permutation(jax.random.fold_in(own, 3), number_of)
    giver, sink = mixed[0:number_of // 2 * 2:2], mixed[1:number_of // 2 * 2:2]
    margin = jnp.minimum(tallies[giver] - 1, bound - tallies[sink]) // 2
    margin = jnp.where((giver == sequence[0]) | (sink == sequence[0]) | (tallies[sink] == 0), 0, jnp.maximum(margin, 0))
    moved = jax.random.randint(jax.random.fold_in(own, 4), (number_of // 2,), 0, 1 << 20) % (margin + 1)
    tallies = tallies.at[giver].add(-moved).at[sink].add(moved)
    labels = jnp.searchsorted(jnp.cumsum(tallies), jnp.arange(rows * top), side="right").astype(jnp.int32)
    grid = labels.reshape(top, rows).T
    grid = grid[jax.random.permutation(jax.random.fold_in(own, 1), rows)]
    offset_by = jax.random.randint(jax.random.fold_in(own, 2), (rows, 1), 0, top)
    return jnp.take_along_axis(grid, (jnp.arange(top)[None, :] + offset_by) % top, axis=1)


def shares(count, total, reach, slope, full):
    portions = [(1 << 20) // math.isqrt(grade ** slope) + 1 for grade in range(1, count + 1)]
    largest = reach if full else min(reach, max(-(-total // count), total * portions[0] // sum(portions)))
    least = 1 if total - largest >= count - 1 else 0
    given, surplus = [largest] + [least] * (count - 1), total - largest - least * (count - 1)
    while surplus > 0:
        movable = [i for i in range(1, count) if given[i] < largest] or [i for i in range(1, count) if given[i] < reach]
        pool, remaining = sum([portions[i] for i in movable]), surplus
        for i in movable:
            more = min(reach - given[i], max(1, remaining * portions[i] // pool), surplus)
            given[i] = given[i] + more
            surplus = surplus - more
    return np.array(given)


def centred(own_key, dims, spread, most, split=(), kind=jnp.bfloat16):
    loudness = levels(own_key, dims, split, -0.22, 0.18) if split else 1.0
    values = jax.random.normal(own_key, dims, jnp.float32) * spread * loudness
    return jnp.minimum(jnp.maximum(values, -most), most).astype(kind)


def setup_inputs(seed: int = 0) -> dict:
    arg_keys = jax.random.split(jax.random.key(seed), 8)
    tokens = centred(arg_keys[0], (SECTIONS, TOKENS, D), 1.0, 6.0, ((0, 2), (1, 16)))
    out_grad = centred(arg_keys[1], (SECTIONS, TOKENS, D), 1.0, 6.0, ((0, 2), (1, 16)))
    probs = jnp.clip(jnp.exp(math.log(0.29882812) - 2.7092764 * jax.random.uniform(arg_keys[2], (SECTIONS, TOKENS, TOPK), jnp.float32) ** levels(arg_keys[2], (SECTIONS, TOKENS, TOPK), ((0, 2), (1, 16)), -0.2, 0.2)), 0.019897461, 0.29882812).astype(jnp.bfloat16)
    expert_ids_keys = jax.random.split(jax.random.fold_in(arg_keys[3], 1), SECTIONS * TOKENS // TOK_DEV)
    expert_ids_turns = jax.random.permutation(jax.random.fold_in(arg_keys[3], 3), SECTIONS * TOKENS // TOK_DEV)
    expert_ids = jax.vmap(lambda own, number: routed_block(jax.random.fold_in(arg_keys[3], 2), own, number, TOK_DEV, EXPERTS, TOPK, CAP, 2))(expert_ids_keys, expert_ids_turns).reshape((SECTIONS, TOKENS, TOPK))
    w_gate = centred(arg_keys[4], (SECTIONS, EXPERTS, FF, D), D ** -0.5, 0.09375, ((0, 2), (1, 16), (2, 8)))
    w_up = centred(arg_keys[5], (SECTIONS, EXPERTS, FF, D), D ** -0.5, 0.09375, ((0, 2), (1, 16), (2, 8)))
    w_down = centred(arg_keys[6], (SECTIONS, EXPERTS, FF, D), FF ** -0.5, 0.15625, ((0, 2), (1, 16), (2, 8)))
    return dict(tokens=tokens, out_grad=out_grad, probs=probs, expert_ids=expert_ids, w_gate=w_gate, w_up=w_up, w_down=w_down)


def slot_table(block_ids, experts, capacity):
    flat_ids = block_ids.reshape(-1).astype(jnp.int32)
    one_hot = (flat_ids[:, None] == jnp.arange(experts, dtype=jnp.int32)[None, :]).astype(jnp.int32)
    before = (jnp.cumsum(one_hot, axis=0) - one_hot).astype(jnp.int32)
    slot_rank = jnp.sum(before * one_hot, axis=1).astype(jnp.int32)
    dest_index = (flat_ids * capacity + slot_rank).astype(jnp.int32)
    count = flat_ids.shape[0]
    anchor = jnp.full((experts * capacity,), count, jnp.int32).at[dest_index].set(jnp.arange(count, dtype=jnp.int32))
    return dest_index, anchor


def expert_rows(rows_in, grads_in, probs_in, gate_mat, up_mat, down_mat):
    total = rows_in.shape[0]
    group = FF // N_DP
    gate_pre = jnp.dot(rows_in, gate_mat.T, preferred_element_type=jnp.float32)
    up_pre = jnp.dot(rows_in, up_mat.T, preferred_element_type=jnp.float32)
    grad_proj = jnp.dot(grads_in, down_mat.T, preferred_element_type=jnp.float32)
    sigma = jax.nn.sigmoid(gate_pre)
    silu_gate = gate_pre * sigma
    hidden = (silu_gate * up_pre).astype(jnp.bfloat16)
    prob_groups = jnp.sum((hidden.astype(jnp.float32) * grad_proj).reshape(total, N_DP, group), axis=2)
    prob_part = jnp.sum(lax.optimization_barrier(prob_groups.astype(jnp.bfloat16)).astype(jnp.float32), axis=1)
    grad_hidden = probs_in[:, None] * grad_proj
    grad_gate_pre = (grad_hidden * up_pre * sigma * (1.0 + gate_pre * (1.0 - sigma))).astype(jnp.bfloat16)
    grad_up_pre = (grad_hidden * silu_gate).astype(jnp.bfloat16)
    scaled_grad = (probs_in[:, None] * grads_in.astype(jnp.float32)).astype(jnp.bfloat16)
    input_groups = jnp.einsum("rjf,jfd->rjd", grad_gate_pre.reshape(total, N_DP, group).astype(jnp.float32), gate_mat.reshape(N_DP, group, D).astype(jnp.float32))
    input_groups = input_groups + jnp.einsum("rjf,jfd->rjd", grad_up_pre.reshape(total, N_DP, group).astype(jnp.float32), up_mat.reshape(N_DP, group, D).astype(jnp.float32))
    input_part = jnp.sum(lax.optimization_barrier(input_groups.astype(jnp.bfloat16)).astype(jnp.float32), axis=1)
    gate_grad = jnp.dot(grad_gate_pre.T, rows_in, preferred_element_type=jnp.float32).astype(jnp.bfloat16)
    up_grad = jnp.dot(grad_up_pre.T, rows_in, preferred_element_type=jnp.float32).astype(jnp.bfloat16)
    down_grad = jnp.dot(hidden.T, scaled_grad, preferred_element_type=jnp.float32).astype(jnp.bfloat16)
    return input_part, prob_part, gate_grad, up_grad, down_grad


def one_section(section_tokens, section_grads, section_probs, section_ids, gate_all, up_all, down_all):
    dest_index, anchor = jax.vmap(lambda block: slot_table(block, EXPERTS, CAP))(section_ids.reshape(N_CP, TOK_DEV, TOPK))
    source_rows = (anchor // TOPK).astype(jnp.int32)
    zero_row = jnp.zeros((N_CP, 1, D), jnp.bfloat16)
    pad_tokens = jnp.concatenate([section_tokens.reshape(N_CP, TOK_DEV, D), zero_row], axis=1)
    pad_grads = jnp.concatenate([section_grads.reshape(N_CP, TOK_DEV, D), zero_row], axis=1)
    pad_probs = jnp.concatenate([section_probs.reshape(N_CP, TOK_DEV * TOPK), jnp.zeros((N_CP, 1), jnp.bfloat16)], axis=1)
    sent_tokens = jax.vmap(lambda table, rows: table[rows])(pad_tokens, source_rows).reshape(N_CP, EXPERTS, CAP, D)
    sent_grads = jax.vmap(lambda table, rows: table[rows])(pad_grads, source_rows).reshape(N_CP, EXPERTS, CAP, D)
    sent_probs = jax.vmap(lambda table, rows: table[rows])(pad_probs, anchor).reshape(N_CP, EXPERTS, CAP)

    def per_expert(expert):
        rows_in = sent_tokens[:, expert].reshape(N_CP * CAP, D)
        grads_in = sent_grads[:, expert].reshape(N_CP * CAP, D)
        probs_in = sent_probs[:, expert].reshape(N_CP * CAP).astype(jnp.float32)
        return expert_rows(rows_in, grads_in, probs_in, gate_all[expert], up_all[expert], down_all[expert])

    input_part, prob_part, gate_grad, up_grad, down_grad = lax.map(per_expert, jnp.arange(EXPERTS, dtype=jnp.int32))
    back_rows = jnp.transpose(input_part.reshape(EXPERTS, N_CP, CAP, D), (1, 0, 2, 3)).reshape(N_CP, EXPERTS * CAP, D)
    back_probs = jnp.transpose(prob_part.reshape(EXPERTS, N_CP, CAP), (1, 0, 2)).reshape(N_CP, EXPERTS * CAP)
    picked = jax.vmap(lambda table, rows: table[rows])(back_rows, dest_index)
    input_grad = jnp.sum(picked.reshape(N_CP, TOK_DEV, TOPK, D), axis=2).reshape(TOKENS, D)
    prob_grad = jax.vmap(lambda table, rows: table[rows])(back_probs, dest_index).reshape(TOKENS, TOPK)
    return input_grad, prob_grad, gate_grad, up_grad, down_grad


def reference(tokens, out_grad, probs, expert_ids, w_gate, w_up, w_down):
    inputs, prob_list, gate_list, up_list, down_list = [], [], [], [], []
    for section in range(SECTIONS):
        result = one_section(tokens[section], out_grad[section], probs[section], expert_ids[section], w_gate[section], w_up[section], w_down[section])
        inputs.append(result[0])
        prob_list.append(result[1])
        gate_list.append(result[2])
        up_list.append(result[3])
        down_list.append(result[4])
    passed = [inputs[section + 1].astype(jnp.bfloat16) for section in range(SECTIONS - 1)]
    passed.append(jnp.zeros((TOKENS, D), jnp.bfloat16))
    return (jnp.stack(passed), jnp.stack(prob_list).astype(jnp.float32), jnp.stack(gate_list), jnp.stack(up_list), jnp.stack(down_list))
```

```python
import jax
import jax.numpy as jnp
from jax import lax
from jax.sharding import PartitionSpec as P

CAP_NUM, CAP_DEN = 5, 4


def body(tokens, out_grad, probs, expert_ids, w_gate, w_up, w_down):
    tok_rows = tokens.shape[1]
    width = tokens.shape[2]
    top_count = probs.shape[2]
    experts = lax.axis_size("cp")
    replicas = lax.axis_size("dp")
    capacity = tok_rows * top_count * CAP_NUM // (CAP_DEN * experts)
    columns = width // replicas
    dp = lax.axis_index("dp")
    me = lax.axis_index("cp")
    own = lax.dynamic_slice_in_dim(
        jnp.stack([tokens[0], out_grad[0]]), dp * columns, columns, 2
    )
    blocks = lax.all_gather(own, "cp")
    ids_all = lax.all_gather(expert_ids[0], "cp")
    probs_all = lax.all_gather(probs[0], "cp")
    match = ids_all == me
    has = jnp.any(match, axis=2)
    prob_tok = jnp.sum(jnp.where(match, probs_all.astype(jnp.float32), 0.0), axis=2)
    has_i = has.astype(jnp.int32)
    slot = jnp.cumsum(has_i, axis=1) - has_i
    pick = (slot[:, None, :] == jnp.arange(capacity)[None, :, None]) & has[:, None, :]
    probs_in = jnp.sum(jnp.where(pick, prob_tok[:, None, :], 0.0), axis=2).reshape(-1, 1)
    rows = jnp.einsum(
        "bct,bstd->sbcd", pick.astype(jnp.bfloat16), blocks, preferred_element_type=jnp.float32
    ).astype(jnp.bfloat16)
    total_rows = experts * capacity
    rows = rows.reshape(2 * total_rows, columns)
    full = lax.all_gather(rows, "dp", axis=1, tiled=True)
    rows_in, grads_in = full[:total_rows], full[total_rows:]
    gate_mat = w_gate[0, 0]
    up_mat = w_up[0, 0]
    down_mat = w_down[0, 0]
    by_feature = (((1,), (1,)), ((), ()))
    by_row = (((0,), (0,)), ((), ()))
    gate_pre = lax.dot_general(rows_in, gate_mat, by_feature, preferred_element_type=jnp.float32)
    up_pre = lax.dot_general(rows_in, up_mat, by_feature, preferred_element_type=jnp.float32)
    grad_proj = lax.dot_general(grads_in, down_mat, by_feature, preferred_element_type=jnp.float32)
    sigma = jax.nn.sigmoid(gate_pre)
    silu_gate = gate_pre * sigma
    hidden = (silu_gate * up_pre).astype(jnp.bfloat16)
    prob_part = jnp.sum(hidden.astype(jnp.float32) * grad_proj, axis=1)
    grad_hidden = probs_in * grad_proj
    grad_gate_pre = (grad_hidden * up_pre * sigma * (1.0 + gate_pre * (1.0 - sigma))).astype(
        jnp.bfloat16
    )
    grad_up_pre = (grad_hidden * silu_gate).astype(jnp.bfloat16)
    scaled_hidden = hidden
    scaled_grad = (probs_in * grads_in).astype(jnp.bfloat16)
    input_part = jnp.dot(grad_gate_pre, gate_mat, preferred_element_type=jnp.float32)
    input_part = (
        input_part + jnp.dot(grad_up_pre, up_mat, preferred_element_type=jnp.float32)
    ).astype(jnp.bfloat16)
    gate_grad = lax.dot_general(
        grad_gate_pre, rows_in, by_row, preferred_element_type=jnp.float32
    ).astype(jnp.bfloat16)
    up_grad = lax.dot_general(
        grad_up_pre, rows_in, by_row, preferred_element_type=jnp.float32
    ).astype(jnp.bfloat16)
    down_grad = lax.dot_general(
        scaled_hidden, scaled_grad, by_row, preferred_element_type=jnp.float32
    ).astype(jnp.bfloat16)
    reduced = lax.psum_scatter(input_part, "dp", scatter_dimension=1, tiled=True)
    back = lax.all_to_all(
        reduced.reshape(experts, capacity, columns), "cp", split_axis=0, concat_axis=0, tiled=True
    )
    back_probs = lax.all_to_all(
        prob_part.reshape(experts, capacity), "cp", split_axis=0, concat_axis=0, tiled=True
    )
    back_probs = lax.psum(back_probs, "dp")
    one_hot = expert_ids[0][:, :, None] == jnp.arange(experts)[None, None, :]
    has_e = jnp.any(one_hot, axis=1).astype(jnp.int32)
    slot_e = jnp.cumsum(has_e, axis=0) - has_e
    pick_e = (slot_e[:, :, None] == jnp.arange(capacity)[None, None, :]) & (has_e[:, :, None] > 0)
    input_sum = jnp.dot(
        pick_e.reshape(tok_rows, total_rows).astype(jnp.bfloat16),
        back.reshape(total_rows, columns),
        preferred_element_type=jnp.float32,
    )
    prob_te = jnp.sum(jnp.where(pick_e, back_probs[None], 0.0), axis=2)
    prob_grad = jnp.sum(jnp.where(one_hot, prob_te[:, None, :], 0.0), axis=2)
    passed = lax.ppermute(input_sum.astype(jnp.bfloat16), "pp", [(1, 0)])
    return (
        passed[None],
        prob_grad[None],
        gate_grad[None, None],
        up_grad[None, None],
        down_grad[None, None],
    )


def solution(mesh):
    in_specs = (
        P("pp", "cp", None),
        P("pp", "cp", None),
        P("pp", "cp", None),
        P("pp", "cp", None),
        P("pp", "cp", "dp", None),
        P("pp", "cp", "dp", None),
        P("pp", "cp", "dp", None),
    )
    out_specs = (
        P("pp", "cp", "dp"),
        P("pp", "cp", None),
        P("pp", "cp", "dp", None),
        P("pp", "cp", "dp", None),
        P("pp", "cp", "dp", None),
    )
    return jax.shard_map(body, mesh=mesh, in_specs=in_specs, out_specs=out_specs, check_vma=False)
```

```python
import functools
import jax
import jax.numpy as jnp
from jax import lax
from jax.experimental import pallas as pl
from jax.experimental.pallas import tpu as pltpu
from jax.sharding import PartitionSpec as P

CAP_NUM, CAP_DEN = 5, 4
MESH = pl.DeviceIdType.MESH
F32, BF16 = jnp.float32, jnp.bfloat16


def expert_kernel(
    dims, tok, grd, ids, prb, w_gate, w_up, w_down,
    ip_out, prob_out, gg_out, ug_out, dg_out,
    blk, stg, xs, wg, wu, wd, hid, ggp, gup, ipb, grb,
    loc, zr, xr, cr, yt, yg, cf, snd, osem,
):
    tok_rows, width, experts, cap, nz, ny = dims
    quarter = width // 4
    route = 16
    pay = 2 * tok_rows + route
    half_pay = tok_rows + route
    dp = lax.axis_index("dp")
    cp = lax.axis_index("cp")
    ndp, ncp = 2 * ny, 2 * nz
    z, xl = cp // 2, cp % 2
    y, core = dp // 2, dp % 2
    half = y % 2
    mine_q = pl.multiple_of((half * 2 + core) * quarter, 128)
    other_q = pl.multiple_of(((1 - half) * 2 + core) * quarter, 128)
    cp_x = z * 2 + (1 - xl)
    dp_c = y * 2 + (1 - core)
    z_up = ((z + 1) % nz) * 2 + xl
    z_dn = ((z + nz - 1) % nz) * 2 + xl
    y_up = ((y + 1) % ny) * 2 + core
    y_dn = ((y + ny - 1) % ny) * 2 + core

    barrier = pltpu.get_barrier_semaphore()
    for where in (
        {"cp": cp_x}, {"cp": z_up}, {"cp": z_dn}, {"dp": dp_c}, {"dp": y_up}, {"dp": y_dn},
    ):
        pl.semaphore_signal(barrier, inc=1, device_id=where, device_id_type=MESH)

    loads = [
        pltpu.make_async_copy(
            tok.at[:, pl.ds(mine_q, quarter)], blk.at[z, pl.ds(0, tok_rows), :], loc.at[0]
        ),
        pltpu.make_async_copy(
            grd.at[:, pl.ds(mine_q, quarter)], blk.at[z, pl.ds(half_pay, tok_rows), :], loc.at[1]
        ),
    ]
    weights = [
        pltpu.make_async_copy(w_gate, wg, loc.at[2]),
        pltpu.make_async_copy(w_up, wu, loc.at[3]),
        pltpu.make_async_copy(w_down, wd, loc.at[4]),
    ]
    for c in loads:
        c.start()
    for c in weights:
        c.start()

    e_iota = lax.broadcasted_iota(jnp.int32, (experts, tok_rows), 0)
    has = jnp.zeros((experts, tok_rows), F32)
    wgt = jnp.zeros((experts, tok_rows), F32)
    id_val = ids[...]
    prb_val = prb[...].astype(F32)
    for k in range(id_val.shape[0]):
        hit = id_val[k : k + 1, :] == e_iota
        has = jnp.where(hit, 1.0, has)
        wgt = jnp.where(hit, prb_val[k : k + 1, :], wgt)
    earlier = (
        lax.broadcasted_iota(jnp.int32, (tok_rows, tok_rows), 0)
        < lax.broadcasted_iota(jnp.int32, (tok_rows, tok_rows), 1)
    )
    slot = jnp.dot(
        has.astype(BF16), jnp.where(earlier, 1.0, 0.0).astype(BF16), preferred_element_type=F32
    )
    slot = jnp.where(has > 0.0, slot, -1.0)
    blk[z, tok_rows:half_pay, :] = jnp.zeros((route, quarter), BF16)
    blk[z, tok_rows:half_pay, 0:tok_rows] = slot.astype(BF16)
    blk[z, tok_rows:half_pay, tok_rows : 2 * tok_rows] = wgt.astype(BF16)
    for c in loads:
        c.wait()
    pl.semaphore_wait(barrier, 6)

    def remote(src, dst, s, r, where):
        return pltpu.make_async_remote_copy(
            src_ref=src, dst_ref=dst, send_sem=s, recv_sem=r, device_id=where, device_id_type=MESH
        )

    first, second = pl.ds(0, half_pay), pl.ds(half_pay, tok_rows)
    s_z, s_x, s_c, s_t, s_g, s_f = (snd.at[j] for j in range(6))

    def z_at(i):
        away = (i + 1) // 2
        return (z + nz + jnp.where(i % 2 == 1, -away, away)) % nz

    def block_rows(zz, kind):
        lane = jnp.where(kind == 0, xl, 1 - xl)
        return pl.multiple_of((zz * 2 + lane) * cap, 16)

    def x_copy(i):
        zz = z_at(i)
        dst = xs.at[:, pl.ds(pl.multiple_of((zz * 2 + xl) * cap, 16), cap), pl.ds(mine_q, quarter)]
        return remote(stg.at[i], dst, s_x, xr.at[i], {"cp": cp_x})

    def share(i, kind):
        unit = kind * nz + i
        rows = pl.ds(block_rows(z_at(i), kind), cap)
        cols = pl.ds(mine_q, quarter)
        piece = xs.at[:, rows, cols]
        top, low = xs.at[0, rows, cols], xs.at[1, rows, cols]
        return (
            remote(piece, piece, s_c, cr.at[unit], {"dp": dp_c}),
            remote(top, top, s_t, yt.at[unit], {"dp": y_up}),
            remote(low, low, s_g, yg.at[unit], {"dp": y_dn}),
        )

    def from_y(i, kind):
        unit = kind * nz + i
        rows = pl.ds(block_rows(z_at(i), kind), cap)
        cols = pl.ds(other_q, quarter)
        piece = xs.at[:, rows, cols]
        top, low = xs.at[0, rows, cols], xs.at[1, rows, cols]
        return (
            remote(top, top, s_t, yt.at[unit], {"dp": y_up}),
            remote(low, low, s_g, yg.at[unit], {"dp": y_dn}),
            remote(piece, piece, s_f, cf.at[unit], {"dp": dp_c}),
        )

    def forward(i, kind):
        got_t, got_g, fwd = from_y(i, kind)
        got_t.wait_recv()
        got_g.wait_recv()
        fwd.start()

    def stage_block(i):
        zz = z_at(i)
        whole = blk.at[zz]

        @pl.when((i >= 1) & (i <= 6))
        def _():
            remote(whole, whole, s_z, zr.at[i], {"cp": z_up}).wait_recv()

        @pl.when(i == 7)
        def _():
            a, b = blk.at[zz, first, :], blk.at[zz, second, :]
            remote(a, a, s_z, zr.at[7], {"cp": z_up}).wait_recv()
            remote(b, b, s_z, zr.at[8], {"cp": z_dn}).wait_recv()

        @pl.when((i == 0) | (i == 1) | (i == 3))
        def _():
            remote(whole, whole, s_z, zr.at[jnp.where(i == 0, 1, i + 2)], {"cp": z_up}).start()

        @pl.when((i == 0) | (i == 2) | (i == 4))
        def _():
            remote(whole, whole, s_z, zr.at[i + 2], {"cp": z_dn}).start()

        @pl.when(i == 5)
        def _():
            a = blk.at[zz, first, :]
            remote(a, a, s_z, zr.at[7], {"cp": z_up}).start()

        @pl.when(i == 6)
        def _():
            b = blk.at[zz, second, :]
            remote(b, b, s_z, zr.at[8], {"cp": z_dn}).start()

        table = blk[zz, tok_rows:half_pay, 0 : 2 * tok_rows].astype(F32)
        slots, probs = table[:, :tok_rows], table[:, tok_rows:]
        c_iota = lax.broadcasted_iota(jnp.int32, (cap, tok_rows), 0).astype(F32)
        plain, scaled = [], []
        for expert in (cp, cp_x):
            sel = e_iota == expert
            s_row = jnp.sum(jnp.where(sel, slots, 0.0), axis=0, keepdims=True)
            p_row = jnp.sum(jnp.where(sel, probs, 0.0), axis=0, keepdims=True)
            hit = c_iota == s_row
            plain.append(jnp.where(hit, 1.0, 0.0).astype(BF16))
            scaled.append(jnp.where(hit, p_row, 0.0).astype(BF16))
        rows = pl.ds(block_rows(zz, 0), cap)
        cols = pl.ds(mine_q, quarter)
        for part, lo, onehots in ((0, 0, plain), (1, half_pay, scaled)):
            data = blk[zz, lo : lo + tok_rows, :]
            both = jnp.dot(
                jnp.concatenate(onehots, axis=0), data, preferred_element_type=F32
            ).astype(BF16)
            xs[part, rows, cols] = both[:cap]
            stg[i, part] = both[cap:]
        x_copy(i).start()
        for c in share(i, 0):
            c.start()

    by_feature = (((1,), (1,)), ((), ()))
    by_row = (((0,), (0,)), ((), ()))
    pair = 2 * cap

    def out_copy(zz, j):
        rows = pl.ds(pl.multiple_of(zz * pair, 16), pair)
        return pltpu.make_async_copy(ipb.at[j], ip_out.at[rows, :], osem.at[j])

    def compute(i):
        zz = z_at(i)
        for kind in (0, 1):
            own, _, _ = share(i, kind)
            own.wait_recv()
            _, _, fwd = from_y(i, kind)
            fwd.wait_recv()
        rows = pl.ds(pl.multiple_of(zz * pair, 16), pair)
        x_rows = xs[0, rows, :]
        gate_pre = lax.dot_general(x_rows, wg[...], by_feature, preferred_element_type=F32)
        up_pre = lax.dot_general(x_rows, wu[...], by_feature, preferred_element_type=F32)
        g_hid = lax.dot_general(xs[1, rows, :], wd[...], by_feature, preferred_element_type=F32)
        sigma = jax.nn.sigmoid(gate_pre)
        silu = gate_pre * sigma
        hidden = (silu * up_pre).astype(BF16)
        hid[rows, :] = hidden
        prob_out[rows, :] = jnp.sum(hidden.astype(F32) * g_hid, axis=1, keepdims=True)
        g_gate = (g_hid * up_pre * sigma * (1.0 + gate_pre * (1.0 - sigma))).astype(BF16)
        g_up = (g_hid * silu).astype(BF16)
        ggp[rows, :] = g_gate
        gup[rows, :] = g_up
        j = i % 2

        @pl.when(i >= 2)
        def _():
            out_copy(zz, j).wait()

        step = 512
        for lo in range(0, width, step):
            part = jnp.dot(g_gate, wg[:, lo : lo + step], preferred_element_type=F32)
            part += jnp.dot(g_up, wu[:, lo : lo + step], preferred_element_type=F32)
            ipb[j, :, lo : lo + step] = part.astype(BF16)
        out_copy(zz, j).start()

    def step_fn(i, carry):
        @pl.when(i < nz)
        def _():
            stage_block(i)

        @pl.when((i >= 1) & (i < nz + 1))
        def _():
            x_copy(i - 1).wait_recv()
            for c in share(i - 1, 1):
                c.start()

        @pl.when((i >= 2) & (i < nz + 2))
        def _():
            forward(i - 2, 0)

        @pl.when((i >= 3) & (i < nz + 3))
        def _():
            forward(i - 3, 1)

        @pl.when(i == 4)
        def _():
            for c in weights:
                c.wait()

        @pl.when(i >= 4)
        def _():
            compute(i - 4)

        return carry

    lax.fori_loop(0, nz + 4, step_fn, 0)

    step = 512
    ff = grb.shape[1]

    def grads(t, carry):
        cols = pl.ds(pl.multiple_of(t * step, 128), step)
        x_cols = xs[0, :, cols]
        grb[0, :, cols] = lax.dot_general(
            ggp[...], x_cols, by_row, preferred_element_type=F32
        ).astype(BF16)
        grb[1, :, cols] = lax.dot_general(
            gup[...], x_cols, by_row, preferred_element_type=F32
        ).astype(BF16)
        grb[2, :, cols] = lax.dot_general(
            hid[...], xs[1, :, cols], by_row, preferred_element_type=F32
        ).astype(BF16)
        return carry

    lax.fori_loop(0, width // step, grads, 0)
    outs = [
        pltpu.make_async_copy(grb.at[j], o, loc.at[j]) for j, o in enumerate((gg_out, ug_out, dg_out))
    ]
    for c in outs:
        c.start()
    cols, ocols = pl.ds(mine_q, quarter), pl.ds(other_q, quarter)
    seven = blk.at[pl.ds(0, nz - 1)]
    remote(seven, seven, s_z, zr.at[0], {"cp": z_up}).wait_send()
    remote(stg, stg, s_x, zr.at[0], {"cp": cp_x}).wait_send()
    a = xs.at[:, :, cols]
    remote(a, a, s_c, zr.at[0], {"dp": dp_c}).wait_send()
    a = xs.at[0, :, cols]
    remote(a, a, s_t, zr.at[0], {"dp": y_up}).wait_send()
    a = xs.at[1, :, cols]
    remote(a, a, s_g, zr.at[0], {"dp": y_dn}).wait_send()
    a = xs.at[:, :, ocols]
    remote(a, a, s_f, zr.at[0], {"dp": dp_c}).wait_send()
    out_copy(z, 0).wait()
    out_copy(z, 1).wait()
    for c in outs:
        c.wait()


def expert_call(tokens, out_grad, ids_t, probs_t, w_gate, w_up, w_down):
    tok_rows, width = tokens.shape
    experts = lax.axis_size("cp")
    nz, ny = experts // 2, lax.axis_size("dp") // 2
    top = ids_t.shape[0]
    cap = tok_rows * top * CAP_NUM // (CAP_DEN * experts)
    ff = w_gate.shape[0]
    rows = experts * cap
    quarter = width // 4
    pay = 2 * tok_rows + 16
    anyspace = pl.BlockSpec(memory_space=pl.ANY)
    vmem = pl.BlockSpec(memory_space=pltpu.VMEM)
    wshape = jax.ShapeDtypeStruct((ff, width), BF16)
    dma = pltpu.SemaphoreType.DMA
    return pl.pallas_call(
        functools.partial(expert_kernel, (tok_rows, width, experts, cap, nz, ny)),
        out_shape=(
            jax.ShapeDtypeStruct((rows, width), BF16),
            jax.ShapeDtypeStruct((rows, 1), F32),
            wshape, wshape, wshape,
        ),
        in_specs=[anyspace, anyspace, vmem, vmem, anyspace, anyspace, anyspace],
        out_specs=(anyspace, vmem, anyspace, anyspace, anyspace),
        scratch_shapes=[
            pltpu.VMEM((nz, pay, quarter), BF16),
            pltpu.VMEM((nz, 2, cap, quarter), BF16),
            pltpu.VMEM((2, rows, width), BF16),
            pltpu.VMEM((ff, width), BF16),
            pltpu.VMEM((ff, width), BF16),
            pltpu.VMEM((ff, width), BF16),
            pltpu.VMEM((rows, ff), BF16),
            pltpu.VMEM((rows, ff), BF16),
            pltpu.VMEM((rows, ff), BF16),
            pltpu.VMEM((2, 2 * cap, width), BF16),
            pltpu.VMEM((3, ff, width), BF16),
            dma((5,)), dma((9,)), dma((nz,)), dma((2 * nz,)), dma((2 * nz,)), dma((2 * nz,)),
            dma((2 * nz,)), dma((6,)), dma((2,)),
        ],
        compiler_params=pltpu.CompilerParams(
            collective_id=0, has_side_effects=True, vmem_limit_bytes=60 * 1024 * 1024
        ),
        name="expert",
    )(tokens, out_grad, ids_t, probs_t, w_gate, w_up, w_down)


def body(tokens, out_grad, probs, expert_ids, w_gate, w_up, w_down):
    tok_rows = tokens.shape[1]
    width = tokens.shape[2]
    top_count = probs.shape[2]
    experts = lax.axis_size("cp")
    replicas = lax.axis_size("dp")
    capacity = tok_rows * top_count * CAP_NUM // (CAP_DEN * experts)
    columns = width // replicas
    total_rows = experts * capacity
    input_part, prob_part, gate_grad, up_grad, down_grad = expert_call(
        tokens[0], out_grad[0], expert_ids[0].T, probs[0].T, w_gate[0, 0], w_up[0, 0], w_down[0, 0]
    )
    reduced = lax.psum_scatter(input_part, "dp", scatter_dimension=1, tiled=True)
    back = lax.all_to_all(
        reduced.reshape(experts, capacity, columns), "cp", split_axis=0, concat_axis=0, tiled=True
    )
    back_probs = lax.all_to_all(
        prob_part.reshape(experts, capacity), "cp", split_axis=0, concat_axis=0, tiled=True
    )
    back_probs = lax.psum(back_probs, "dp")
    one_hot = expert_ids[0][:, :, None] == jnp.arange(experts)[None, None, :]
    has_e = jnp.any(one_hot, axis=1).astype(jnp.int32)
    slot_e = jnp.cumsum(has_e, axis=0) - has_e
    pick_e = (slot_e[:, :, None] == jnp.arange(capacity)[None, None, :]) & (has_e[:, :, None] > 0)
    input_sum = jnp.dot(
        pick_e.reshape(tok_rows, total_rows).astype(jnp.bfloat16),
        back.reshape(total_rows, columns),
        preferred_element_type=jnp.float32,
    )
    prob_te = jnp.sum(jnp.where(pick_e, back_probs[None], 0.0), axis=2)
    prob_grad = jnp.sum(jnp.where(one_hot, prob_te[:, None, :], 0.0), axis=2)
    prob_grad = prob_grad / probs[0].astype(F32)
    passed = lax.ppermute(input_sum.astype(jnp.bfloat16), "pp", [(1, 0)])
    return (
        passed[None],
        prob_grad[None],
        gate_grad[None, None],
        up_grad[None, None],
        down_grad[None, None],
    )


def solution(mesh):
    in_specs = (
        P("pp", "cp", None),
        P("pp", "cp", None),
        P("pp", "cp", None),
        P("pp", "cp", None),
        P("pp", "cp", "dp", None),
        P("pp", "cp", "dp", None),
        P("pp", "cp", "dp", None),
    )
    out_specs = (
        P("pp", "cp", "dp"),
        P("pp", "cp", None),
        P("pp", "cp", "dp", None),
        P("pp", "cp", "dp", None),
        P("pp", "cp", "dp", None),
    )
    return jax.shard_map(body, mesh=mesh, in_specs=in_specs, out_specs=out_specs, check_vma=False)
```

```python
import functools
import jax
import jax.numpy as jnp
from jax import lax
from jax.experimental import pallas as pl
from jax.experimental.pallas import tpu as pltpu
from jax.sharding import PartitionSpec as P

CAP_NUM, CAP_DEN = 5, 4
MESH = pl.DeviceIdType.MESH
F32, BF16 = jnp.float32, jnp.bfloat16


def expert_kernel(
    dims, tok, grd, ids, prb, w_gate, w_up, w_down,
    passed_out, prob_out, gg_out, ug_out, dg_out,
    blk, stg, xs, wg, wu, wd, hid, ggp, gup, grb, ipb, c1r, farr, comr, dirr, l3r,
    ptab, prcv, pcol, pfin, fxs, fxr, fin, zero,
    loc, zr, xr, cr, yt, yg, cf, snd, c1m, fam, com, dim, l3m, ppm, pcm, psn, one,
):
    tok_rows, width, experts, cap, nz, ny = dims
    quarter = width // 4
    route = 16
    pay = 2 * tok_rows + route
    half_pay = tok_rows + route
    dp = lax.axis_index("dp")
    cp = lax.axis_index("cp")
    ndp, ncp = 2 * ny, 2 * nz
    z, xl = cp // 2, cp % 2
    y, core = dp // 2, dp % 2
    half = y % 2
    mine_q = pl.multiple_of((half * 2 + core) * quarter, 128)
    other_q = pl.multiple_of(((1 - half) * 2 + core) * quarter, 128)
    cp_x = z * 2 + (1 - xl)
    dp_c = y * 2 + (1 - core)
    z_up = ((z + 1) % nz) * 2 + xl
    z_dn = ((z + nz - 1) % nz) * 2 + xl
    y_up = ((y + 1) % ny) * 2 + core
    y_dn = ((y + ny - 1) % ny) * 2 + core

    pp = lax.axis_index("pp")
    returns = pp == 1
    same = core == xl
    owner_dp = y * 2 + xl

    def owner(zz):
        return {"cp": zz * 2 + core, "dp": owner_dp}

    barrier = pltpu.get_barrier_semaphore()
    for where in (
        {"cp": cp_x}, {"cp": z_up}, {"cp": z_dn}, {"dp": dp_c}, {"dp": y_up}, {"dp": y_dn},
        {"pp": 1 - pp},
    ):
        pl.semaphore_signal(barrier, inc=1, device_id=where, device_id_type=MESH)
    for dz in range(1, nz):
        pl.semaphore_signal(barrier, inc=1, device_id=owner((z + dz) % nz), device_id_type=MESH)

    @pl.when(jnp.logical_not(same))
    def _():
        pl.semaphore_signal(barrier, inc=1, device_id=owner(z), device_id_type=MESH)

    loads = [
        pltpu.make_async_copy(
            tok.at[:, pl.ds(mine_q, quarter)], blk.at[z, pl.ds(0, tok_rows), :], loc.at[0]
        ),
        pltpu.make_async_copy(
            grd.at[:, pl.ds(mine_q, quarter)], blk.at[z, pl.ds(half_pay, tok_rows), :], loc.at[1]
        ),
    ]
    weights = [
        pltpu.make_async_copy(w_gate, wg, loc.at[2]),
        pltpu.make_async_copy(w_up, wu, loc.at[3]),
        pltpu.make_async_copy(w_down, wd, loc.at[4]),
    ]
    for c in loads:
        c.start()
    for c in weights:
        c.start()

    e_iota = lax.broadcasted_iota(jnp.int32, (experts, tok_rows), 0)
    has = jnp.zeros((experts, tok_rows), F32)
    wgt = jnp.zeros((experts, tok_rows), F32)
    id_val = ids[...]
    prb_val = prb[...].astype(F32)
    for k in range(id_val.shape[0]):
        hit = id_val[k : k + 1, :] == e_iota
        has = jnp.where(hit, 1.0, has)
        wgt = jnp.where(hit, prb_val[k : k + 1, :], wgt)
    earlier = (
        lax.broadcasted_iota(jnp.int32, (tok_rows, tok_rows), 0)
        < lax.broadcasted_iota(jnp.int32, (tok_rows, tok_rows), 1)
    )
    slot = jnp.dot(
        has.astype(BF16), jnp.where(earlier, 1.0, 0.0).astype(BF16), preferred_element_type=F32
    )
    slot = jnp.where(has > 0.0, slot, -1.0)
    blk[z, tok_rows:half_pay, :] = jnp.zeros((route, quarter), BF16)
    blk[z, tok_rows:half_pay, 0:tok_rows] = slot.astype(BF16)
    blk[z, tok_rows:half_pay, tok_rows : 2 * tok_rows] = wgt.astype(BF16)
    for c in loads:
        c.wait()
    ptab[...] = jnp.zeros_like(ptab)
    zero[...] = jnp.zeros_like(zero)
    pl.semaphore_wait(barrier, 7 + nz - 1 + jnp.where(same, 0, 1))

    def remote(src, dst, s, r, where):
        return pltpu.make_async_remote_copy(
            src_ref=src, dst_ref=dst, send_sem=s, recv_sem=r, device_id=where, device_id_type=MESH
        )

    first, second = pl.ds(0, half_pay), pl.ds(half_pay, tok_rows)
    s_z, s_x, s_c, s_t, s_g, s_f = (snd.at[j] for j in range(6))

    def z_at(i):
        away = (i + 1) // 2
        return (z + nz + jnp.where(i % 2 == 1, -away, away)) % nz

    def block_rows(zz, kind):
        lane = jnp.where(kind == 0, xl, 1 - xl)
        return pl.multiple_of((zz * 2 + lane) * cap, 16)

    def x_copy(i):
        zz = z_at(i)
        dst = xs.at[:, pl.ds(pl.multiple_of((zz * 2 + xl) * cap, 16), cap), pl.ds(mine_q, quarter)]
        return remote(stg.at[i], dst, s_x, xr.at[i], {"cp": cp_x})

    def share(i, kind):
        unit = kind * nz + i
        rows = pl.ds(block_rows(z_at(i), kind), cap)
        cols = pl.ds(mine_q, quarter)
        piece = xs.at[:, rows, cols]
        top, low = xs.at[0, rows, cols], xs.at[1, rows, cols]
        return (
            remote(piece, piece, s_c, cr.at[unit], {"dp": dp_c}),
            remote(top, top, s_t, yt.at[unit], {"dp": y_up}),
            remote(low, low, s_g, yg.at[unit], {"dp": y_dn}),
        )

    def from_y(i, kind):
        unit = kind * nz + i
        rows = pl.ds(block_rows(z_at(i), kind), cap)
        cols = pl.ds(other_q, quarter)
        piece = xs.at[:, rows, cols]
        top, low = xs.at[0, rows, cols], xs.at[1, rows, cols]
        return (
            remote(top, top, s_t, yt.at[unit], {"dp": y_up}),
            remote(low, low, s_g, yg.at[unit], {"dp": y_dn}),
            remote(piece, piece, s_f, cf.at[unit], {"dp": dp_c}),
        )

    def forward(i, kind):
        got_t, got_g, fwd = from_y(i, kind)
        got_t.wait_recv()
        got_g.wait_recv()
        fwd.start()

    def stage_block(i):
        zz = z_at(i)
        whole = blk.at[zz]

        @pl.when((i >= 1) & (i <= 6))
        def _():
            remote(whole, whole, s_z, zr.at[i], {"cp": z_up}).wait_recv()

        @pl.when(i == 7)
        def _():
            a, b = blk.at[zz, first, :], blk.at[zz, second, :]
            remote(a, a, s_z, zr.at[7], {"cp": z_up}).wait_recv()
            remote(b, b, s_z, zr.at[8], {"cp": z_dn}).wait_recv()

        @pl.when((i == 0) | (i == 1) | (i == 3))
        def _():
            remote(whole, whole, s_z, zr.at[jnp.where(i == 0, 1, i + 2)], {"cp": z_up}).start()

        @pl.when((i == 0) | (i == 2) | (i == 4))
        def _():
            remote(whole, whole, s_z, zr.at[i + 2], {"cp": z_dn}).start()

        @pl.when(i == 5)
        def _():
            a = blk.at[zz, first, :]
            remote(a, a, s_z, zr.at[7], {"cp": z_up}).start()

        @pl.when(i == 6)
        def _():
            b = blk.at[zz, second, :]
            remote(b, b, s_z, zr.at[8], {"cp": z_dn}).start()

        table = blk[zz, tok_rows:half_pay, 0 : 2 * tok_rows].astype(F32)
        slots, probs = table[:, :tok_rows], table[:, tok_rows:]
        c_iota = lax.broadcasted_iota(jnp.int32, (cap, tok_rows), 0).astype(F32)
        plain, scaled = [], []
        for expert in (cp, cp_x):
            sel = e_iota == expert
            s_row = jnp.sum(jnp.where(sel, slots, 0.0), axis=0, keepdims=True)
            p_row = jnp.sum(jnp.where(sel, probs, 0.0), axis=0, keepdims=True)
            hit = c_iota == s_row
            plain.append(jnp.where(hit, 1.0, 0.0).astype(BF16))
            scaled.append(jnp.where(hit, p_row, 0.0).astype(BF16))
        rows = pl.ds(block_rows(zz, 0), cap)
        cols = pl.ds(mine_q, quarter)
        for part, lo, onehots in ((0, 0, plain), (1, half_pay, scaled)):
            data = blk[zz, lo : lo + tok_rows, :]
            both = jnp.dot(
                jnp.concatenate(onehots, axis=0), data, preferred_element_type=F32
            ).astype(BF16)
            xs[part, rows, cols] = both[:cap]
            stg[i, part] = both[cap:]
        x_copy(i).start()
        for c in share(i, 0):
            c.start()

    by_feature = (((1,), (1,)), ((), ()))
    by_row = (((0,), (0,)), ((), ()))
    pair = 2 * cap

    chunk = width // ny
    half_w = chunk // 2

    def ccols(yy):
        return pl.ds(pl.multiple_of(yy * chunk, 128), chunk)

    def mine_of(i):
        return ipb.at[i, pl.ds(pl.multiple_of(core * cap, 16), cap)]

    def core_sum(i):
        src = ipb.at[i, pl.ds(pl.multiple_of((1 - core) * cap, 16), cap)]
        return remote(src, c1r.at[i], snd.at[6], c1m.at[i], {"dp": dp_c})

    def y_steps(i):
        up = i % 2 == 0
        fwd_y = jnp.where(up, (y + 1) % ny, (y + ny - 1) % ny)
        bwd_y = jnp.where(up, (y + ny - 1) % ny, (y + 1) % ny)
        fwd_to, bwd_to = {"dp": fwd_y * 2 + core}, {"dp": bwd_y * 2 + core}
        rows = pl.ds(pl.multiple_of(core * cap, 16), cap)
        s_y = snd.at[7]
        far = remote(
            ipb.at[i, rows, ccols((y + 2) % ny)], farr.at[i], s_y, fam.at[i], fwd_to
        )
        comb = remote(ipb.at[i, rows, ccols(fwd_y)], comr.at[i], s_y, com.at[i], fwd_to)
        direct = remote(ipb.at[i, rows, ccols(bwd_y)], dirr.at[i], s_y, dim.at[i], bwd_to)
        return far, comb, direct, fwd_y, rows

    def owner_copy(i):
        rows = pl.ds(pl.multiple_of(core * cap, 16), cap)
        return remote(
            ipb.at[i, rows, ccols(y)], l3r.at[z], snd.at[8], l3m.at[z], owner(z_at(i))
        )

    def ret_a(i):
        core_sum(i).wait_recv()
        rows = pl.ds(pl.multiple_of(core * cap, 16), cap)
        ipb[i, rows, :] = (ipb[i, rows, :].astype(F32) + c1r[i].astype(F32)).astype(BF16)
        far, _, direct, _, _ = y_steps(i)
        far.start()
        direct.start()

    def ret_b(i):
        far, comb, _, fwd_y, rows = y_steps(i)
        far.wait_recv()
        cols = ccols(fwd_y)
        ipb[i, rows, cols] = (ipb[i, rows, cols].astype(F32) + farr[i].astype(F32)).astype(BF16)
        comb.start()

    def ret_c(i):
        _, comb, direct, _, rows = y_steps(i)
        comb.wait_recv()
        direct.wait_recv()
        total = ipb[i, rows, ccols(y)].astype(F32) + comr[i].astype(F32) + dirr[i].astype(F32)
        here = same & (i == 0)

        @pl.when(here)
        def _():
            l3r[z] = total.astype(BF16)

        @pl.when(jnp.logical_not(here))
        def _():
            ipb[i, rows, ccols(y)] = total.astype(BF16)
            owner_copy(i).start()

    def compute(i):
        zz = z_at(i)
        for kind in (0, 1):
            own, _, _ = share(i, kind)
            own.wait_recv()
            _, _, fwd = from_y(i, kind)
            fwd.wait_recv()
        rows = pl.ds(pl.multiple_of(zz * pair, 16), pair)
        x_rows = xs[0, rows, :]
        gate_pre = lax.dot_general(x_rows, wg[...], by_feature, preferred_element_type=F32)
        up_pre = lax.dot_general(x_rows, wu[...], by_feature, preferred_element_type=F32)
        g_hid = lax.dot_general(xs[1, rows, :], wd[...], by_feature, preferred_element_type=F32)
        sigma = jax.nn.sigmoid(gate_pre)
        silu = gate_pre * sigma
        hidden = (silu * up_pre).astype(BF16)
        hid[rows, :] = hidden
        prod = hidden.astype(F32) * g_hid
        high = prod.astype(BF16)
        low = (prod - high.astype(F32)).astype(BF16)
        ones = jnp.ones((8, prod.shape[1]), BF16)
        for k in (0, 1):
            part = slice(k * cap, (k + 1) * cap)
            sums = lax.dot_general(ones, high[part], by_feature, preferred_element_type=F32)
            sums += lax.dot_general(ones, low[part], by_feature, preferred_element_type=F32)
            ptab[0, zz * 2 + k, :, 0:cap] = sums
        g_gate = (g_hid * up_pre * sigma * (1.0 + gate_pre * (1.0 - sigma))).astype(BF16)
        g_up = (g_hid * silu).astype(BF16)
        ggp[rows, :] = g_gate
        gup[rows, :] = g_up

        @pl.when(returns)
        def _():
            step = 512
            for lo in range(0, width, step):
                part = jnp.dot(g_gate, wg[:, lo : lo + step], preferred_element_type=F32)
                part += jnp.dot(g_up, wu[:, lo : lo + step], preferred_element_type=F32)
                ipb[i, :, lo : lo + step] = part.astype(BF16)
            core_sum(i).start()

    def pair_copy(r):
        to = (dp_c, (y + 1 - 2 * (y % 2)) * 2 + core, (ny - 1 - y) * 2 + core)[r]
        return remote(ptab.at[r], prcv.at[r], psn.at[r], ppm.at[r], {"dp": to})

    def pair_sum(r):
        pair_copy(r).wait_recv()
        ptab[r + 1] = ptab[r] + prcv[r]

    def prob_copy(dz):
        zz = (z + dz) % nz
        return remote(
            ptab.at[3, zz * 2 + core], pcol.at[z], psn.at[3], pcm.at[z], owner(zz)
        )

    def prob_spread():
        for dz in range(1, nz):
            prob_copy(dz).start()

        @pl.when(jnp.logical_not(same))
        def _():
            prob_copy(0).start()

        @pl.when(same)
        def _():
            pcol[z] = ptab[3, z * 2 + core]

    def own_hits(zz):
        table = blk[z, tok_rows:half_pay, 0:tok_rows].astype(F32)
        row = jnp.sum(jnp.where(e_iota == zz * 2 + core, table, 0.0), axis=0, keepdims=True)
        c_iota = lax.broadcasted_iota(jnp.int32, (cap, tok_rows), 0).astype(F32)
        return jnp.where(c_iota == row, 1.0, 0.0).astype(BF16)

    def each_source(ref, sems, sem):
        for dz in range(1, nz):
            src = (z + dz) % nz
            remote(ref.at[src], ref.at[src], sem, sems.at[src], owner(z)).wait_recv()

        @pl.when(jnp.logical_not(same))
        def _():
            remote(ref.at[z], ref.at[z], sem, sems.at[z], owner(z)).wait_recv()

    last_copy = remote(pfin.at[0], pfin.at[1], psn.at[4], one.at[0], {"dp": dp_c})

    def prob_pick():
        each_source(pcol, pcm, psn.at[3])
        acc = jnp.zeros(id_val.shape, F32)
        for zz in range(nz):
            val = pcol[zz][:, 0:cap]
            high = val.astype(BF16)
            low = (val - high.astype(F32)).astype(BF16)
            hits = own_hits(zz)
            got = jnp.dot(high, hits, preferred_element_type=F32)
            got += jnp.dot(low, hits, preferred_element_type=F32)
            acc = jnp.where(ids[...] == zz * 2 + core, got, acc)
        pfin[0] = acc
        last_copy.start()

    grad_step = 512
    n_grad = width // grad_step

    def grads(t):
        cols = pl.ds(pl.multiple_of(t * grad_step, 128), grad_step)
        x_cols = xs[0, :, cols]
        grb[0, :, cols] = lax.dot_general(
            ggp[...], x_cols, by_row, preferred_element_type=F32
        ).astype(BF16)
        grb[1, :, cols] = lax.dot_general(
            gup[...], x_cols, by_row, preferred_element_type=F32
        ).astype(BF16)
        grb[2, :, cols] = lax.dot_general(
            hid[...], xs[1, :, cols], by_row, preferred_element_type=F32
        ).astype(BF16)

    def step_fn(i, carry):
        @pl.when(i < nz)
        def _():
            stage_block(i)

        @pl.when((i >= 1) & (i < nz + 1))
        def _():
            x_copy(i - 1).wait_recv()
            for c in share(i - 1, 1):
                c.start()

        @pl.when((i >= 2) & (i < nz + 2))
        def _():
            forward(i - 2, 0)

        @pl.when((i >= 3) & (i < nz + 3))
        def _():
            forward(i - 3, 1)

        @pl.when(i == 4)
        def _():
            for c in weights:
                c.wait()

        for lag, stage in ((9, ret_c), (7, ret_b), (5, ret_a)):

            @pl.when(returns & (i >= lag) & (i < nz + lag))
            def _(lag=lag, stage=stage):
                stage(i - lag)

        @pl.when((i >= 4) & (i < nz + 4))
        def _():
            compute(i - 4)

        first_free = nz + 4

        @pl.when(i == first_free)
        def _():
            pair_copy(0).start()

        for r in (0, 1):

            @pl.when(i == first_free + 1 + r)
            def _(r=r):
                pair_sum(r)
                pair_copy(r + 1).start()

        @pl.when(i == first_free + 3)
        def _():
            pair_sum(2)
            prob_spread()

        @pl.when(i == first_free + 5)
        def _():
            prob_pick()

        @pl.when(i >= first_free)
        def _():
            grads(i - first_free)

        return carry

    lax.fori_loop(0, nz + 4 + n_grad, step_fn, 0)

    outs = [
        pltpu.make_async_copy(grb.at[j], o, loc.at[j]) for j, o in enumerate((gg_out, ug_out, dg_out))
    ]
    for c in outs:
        c.start()
    hand_over = remote(fin, passed_out, snd.at[9], one.at[1], {"pp": 0})
    swap = remote(fxs, fxr, snd.at[10], one.at[2], {"dp": dp_c})
    blank = pltpu.make_async_copy(zero, passed_out, loc.at[3])

    @pl.when(returns)
    def _():
        blank.start()
        each_source(l3r, l3m, snd.at[8])
        hits = jnp.concatenate([own_hits(zz) for zz in range(nz)], axis=0)
        rows = jnp.concatenate([l3r[zz] for zz in range(nz)], axis=0)
        tot = lax.dot_general(hits, rows, by_row, preferred_element_type=F32).T

        @pl.when(core == 0)
        def _():
            fxs[...] = tot[half_w:]

        @pl.when(core == 1)
        def _():
            fxs[...] = tot[:half_w]

        swap.start()
        kept = jnp.where(core == 0, tot[:half_w], tot[half_w:])
        swap.wait_recv()
        fin[...] = (kept + fxr[...]).astype(BF16)
        hand_over.start()

    last_copy.wait_recv()
    prob_out[...] = (pfin[0] + pfin[1]) / prb[...].astype(F32)
    cols, ocols = pl.ds(mine_q, quarter), pl.ds(other_q, quarter)
    seven = blk.at[pl.ds(0, nz - 1)]
    remote(seven, seven, s_z, zr.at[0], {"cp": z_up}).wait_send()
    remote(stg, stg, s_x, zr.at[0], {"cp": cp_x}).wait_send()
    a = xs.at[:, :, cols]
    remote(a, a, s_c, zr.at[0], {"dp": dp_c}).wait_send()
    a = xs.at[0, :, cols]
    remote(a, a, s_t, zr.at[0], {"dp": y_up}).wait_send()
    a = xs.at[1, :, cols]
    remote(a, a, s_g, zr.at[0], {"dp": y_dn}).wait_send()
    a = xs.at[:, :, ocols]
    remote(a, a, s_f, zr.at[0], {"dp": dp_c}).wait_send()
    for r in (0, 1, 2):
        pair_copy(r).wait_send()
    last_copy.wait_send()
    seven_p = pcol.at[pl.ds(0, nz - 1)]

    @pl.when(same)
    def _():
        remote(seven_p, seven_p, psn.at[3], one.at[0], owner(z)).wait_send()

    @pl.when(jnp.logical_not(same))
    def _():
        remote(pcol, pcol, psn.at[3], one.at[0], owner(z)).wait_send()

    @pl.when(returns)
    def _():
        remote(c1r, c1r, snd.at[6], one.at[0], {"dp": dp_c}).wait_send()
        total = farr.shape[0] * 3 * chunk // (2 * width)
        sent = ipb.at[pl.ds(0, total)]
        remote(sent, sent, snd.at[7], one.at[0], {"dp": y_up}).wait_send()
        swap.wait_send()
        hand_over.wait_send()
        blank.wait()

    seven_l = l3r.at[pl.ds(0, nz - 1)]

    @pl.when(returns & same)
    def _():
        remote(seven_l, seven_l, snd.at[8], one.at[0], owner(z)).wait_send()

    @pl.when(returns & jnp.logical_not(same))
    def _():
        remote(l3r, l3r, snd.at[8], one.at[0], owner(z)).wait_send()

    @pl.when(jnp.logical_not(returns))
    def _():
        hand_over.wait_recv()

    for c in outs:
        c.wait()


def expert_call(tokens, out_grad, ids_t, probs_t, w_gate, w_up, w_down):
    tok_rows, width = tokens.shape
    experts = lax.axis_size("cp")
    nz, ny = experts // 2, lax.axis_size("dp") // 2
    top = ids_t.shape[0]
    cap = tok_rows * top * CAP_NUM // (CAP_DEN * experts)
    ff = w_gate.shape[0]
    rows = experts * cap
    quarter = width // 4
    pay = 2 * tok_rows + 16
    anyspace = pl.BlockSpec(memory_space=pl.ANY)
    vmem = pl.BlockSpec(memory_space=pltpu.VMEM)
    wshape = jax.ShapeDtypeStruct((ff, width), BF16)
    dma = pltpu.SemaphoreType.DMA
    return pl.pallas_call(
        functools.partial(expert_kernel, (tok_rows, width, experts, cap, nz, ny)),
        out_shape=(
            jax.ShapeDtypeStruct((width // (2 * ny), tok_rows), BF16),
            jax.ShapeDtypeStruct((top, tok_rows), F32),
            wshape, wshape, wshape,
        ),
        in_specs=[anyspace, anyspace, vmem, vmem, anyspace, anyspace, anyspace],
        out_specs=(anyspace, vmem, anyspace, anyspace, anyspace),
        scratch_shapes=[
            pltpu.VMEM((nz, pay, quarter), BF16),
            pltpu.VMEM((nz, 2, cap, quarter), BF16),
            pltpu.VMEM((2, rows, width), BF16),
            pltpu.VMEM((ff, width), BF16),
            pltpu.VMEM((ff, width), BF16),
            pltpu.VMEM((ff, width), BF16),
            pltpu.VMEM((rows, ff), BF16),
            pltpu.VMEM((rows, ff), BF16),
            pltpu.VMEM((rows, ff), BF16),
            pltpu.VMEM((3, ff, width), BF16),
            pltpu.VMEM((nz, 2 * cap, width), BF16),
            pltpu.VMEM((nz, cap, width), BF16),
            pltpu.VMEM((nz, cap, width // ny), BF16),
            pltpu.VMEM((nz, cap, width // ny), BF16),
            pltpu.VMEM((nz, cap, width // ny), BF16),
            pltpu.VMEM((nz, cap, width // ny), BF16),
            pltpu.VMEM((4, experts, 8, 128), F32),
            pltpu.VMEM((3, experts, 8, 128), F32),
            pltpu.VMEM((nz, 8, 128), F32),
            pltpu.VMEM((2, top, tok_rows), F32),
            pltpu.VMEM((width // (2 * ny), tok_rows), F32),
            pltpu.VMEM((width // (2 * ny), tok_rows), F32),
            pltpu.VMEM((width // (2 * ny), tok_rows), BF16),
            pltpu.VMEM((width // (2 * ny), tok_rows), BF16),
            dma((5,)), dma((9,)), dma((nz,)), dma((2 * nz,)), dma((2 * nz,)), dma((2 * nz,)),
            dma((2 * nz,)), dma((11,)), dma((nz,)), dma((nz,)), dma((nz,)), dma((nz,)), dma((nz,)),
            dma((3,)), dma((nz,)), dma((5,)), dma((3,)),
        ],
        compiler_params=pltpu.CompilerParams(
            collective_id=0, has_side_effects=True, vmem_limit_bytes=60 * 1024 * 1024
        ),
        name="expert",
    )(tokens, out_grad, ids_t, probs_t, w_gate, w_up, w_down)


def body(tokens, out_grad, probs, expert_ids, w_gate, w_up, w_down):
    passed, prob_grad, gate_grad, up_grad, down_grad = expert_call(
        tokens[0], out_grad[0], expert_ids[0].T, probs[0].T, w_gate[0, 0], w_up[0, 0], w_down[0, 0]
    )
    return (
        passed.T[None],
        prob_grad.T[None],
        gate_grad[None, None],
        up_grad[None, None],
        down_grad[None, None],
    )


def solution(mesh):
    in_specs = (
        P("pp", "cp", None),
        P("pp", "cp", None),
        P("pp", "cp", None),
        P("pp", "cp", None),
        P("pp", "cp", "dp", None),
        P("pp", "cp", "dp", None),
        P("pp", "cp", "dp", None),
    )
    out_specs = (
        P("pp", "cp", "dp"),
        P("pp", "cp", None),
        P("pp", "cp", "dp", None),
        P("pp", "cp", "dp", None),
        P("pp", "cp", "dp", None),
    )
    return jax.shard_map(body, mesh=mesh, in_specs=in_specs, out_specs=out_specs, check_vma=False)
```

```python
import functools
import jax
import jax.numpy as jnp
from jax import lax
from jax.experimental import pallas as pl
from jax.experimental.pallas import tpu as pltpu
from jax.sharding import PartitionSpec as P

CAP_NUM, CAP_DEN = 5, 4
MESH = pl.DeviceIdType.MESH
PROXIED = 3
F32, BF16 = jnp.float32, jnp.bfloat16


def expert_kernel(
    dims, tok, grd, ids, prb, w_gate, w_up, w_down,
    passed_out, prob_out, gg_out, ug_out, dg_out,
    blk, stg, xs, wg, wu, wd, hid, ggp, gup, grb, ipb, c1r, farr, comr, dirr, l3r,
    ptab, prcv, pcol, pfin, fxs, fxr, tab,
    loc, zr, xr, cr, yt, yg, cf, snd, c1m, fam, com, dim, l3m, pxm, ppm, pcm, psn, one,
):
    tok_rows, width, experts, cap, nz, ny = dims
    quarter = width // 4
    route = 16
    pay = 2 * tok_rows + route
    half_pay = tok_rows + route
    dp = lax.axis_index("dp")
    cp = lax.axis_index("cp")
    ndp, ncp = 2 * ny, 2 * nz
    z, xl = cp // 2, cp % 2
    y, core = dp // 2, dp % 2
    half = y % 2
    mine_q = pl.multiple_of((half * 2 + core) * quarter, 128)
    other_q = pl.multiple_of(((1 - half) * 2 + core) * quarter, 128)
    cp_x = z * 2 + (1 - xl)
    dp_c = y * 2 + (1 - core)
    z_up = ((z + 1) % nz) * 2 + xl
    z_dn = ((z + nz - 1) % nz) * 2 + xl
    y_up = ((y + 1) % ny) * 2 + core
    y_dn = ((y + ny - 1) % ny) * 2 + core

    pp = lax.axis_index("pp")
    returns = pp == 1
    same = core == xl
    owner_dp = y * 2 + xl

    def owner(zz):
        return {"cp": zz * 2 + core, "dp": owner_dp}

    def other_owner(zz):
        return {"pp": 1 - pp, "cp": zz * 2 + core, "dp": owner_dp}

    proxy = {"pp": 1 - pp, "cp": cp_x}

    barrier = pltpu.get_barrier_semaphore()
    for where in (
        {"cp": cp_x}, {"cp": z_up}, {"cp": z_dn}, {"dp": dp_c}, {"dp": y_up}, {"dp": y_dn},
        {"pp": 1 - pp}, proxy,
    ):
        pl.semaphore_signal(barrier, inc=1, device_id=where, device_id_type=MESH)
    for dz in range(nz):
        zz = (z + dz) % nz
        pl.semaphore_signal(barrier, inc=1, device_id=other_owner(zz), device_id_type=MESH)
        if dz:
            pl.semaphore_signal(barrier, inc=1, device_id=owner(zz), device_id_type=MESH)

    @pl.when(jnp.logical_not(same))
    def _():
        pl.semaphore_signal(barrier, inc=1, device_id=owner(z), device_id_type=MESH)

    loads = [
        pltpu.make_async_copy(
            tok.at[:, pl.ds(mine_q, quarter)], blk.at[z, pl.ds(0, tok_rows), :], loc.at[0]
        ),
        pltpu.make_async_copy(
            grd.at[:, pl.ds(mine_q, quarter)], blk.at[z, pl.ds(half_pay, tok_rows), :], loc.at[1]
        ),
    ]
    weights = [
        pltpu.make_async_copy(w_gate, wg, loc.at[2]),
        pltpu.make_async_copy(w_up, wu, loc.at[3]),
        pltpu.make_async_copy(w_down, wd, loc.at[4]),
    ]
    for c in loads:
        c.start()
    for c in weights:
        c.start()

    e_iota = lax.broadcasted_iota(jnp.int32, (experts, tok_rows), 0)
    has = jnp.zeros((experts, tok_rows), F32)
    wgt = jnp.zeros((experts, tok_rows), F32)
    id_val = ids[...]
    prb_val = prb[...].astype(F32)
    for k in range(id_val.shape[0]):
        hit = id_val[k : k + 1, :] == e_iota
        has = jnp.where(hit, 1.0, has)
        wgt = jnp.where(hit, prb_val[k : k + 1, :], wgt)
    earlier = (
        lax.broadcasted_iota(jnp.int32, (tok_rows, tok_rows), 0)
        < lax.broadcasted_iota(jnp.int32, (tok_rows, tok_rows), 1)
    )
    slot = jnp.dot(
        has.astype(BF16), jnp.where(earlier, 1.0, 0.0).astype(BF16), preferred_element_type=F32
    )
    slot = jnp.where(has > 0.0, slot, -1.0)
    blk[z, tok_rows:half_pay, :] = jnp.zeros((route, quarter), BF16)
    blk[z, tok_rows:half_pay, 0:tok_rows] = slot.astype(BF16)
    blk[z, tok_rows:half_pay, tok_rows : 2 * tok_rows] = wgt.astype(BF16)
    for c in loads:
        c.wait()
    ptab[...] = jnp.zeros_like(ptab)
    pl.semaphore_wait(barrier, 8 + 2 * nz - 1 + jnp.where(same, 0, 1))

    def remote(src, dst, s, r, where):
        return pltpu.make_async_remote_copy(
            src_ref=src, dst_ref=dst, send_sem=s, recv_sem=r, device_id=where, device_id_type=MESH
        )

    first, second = pl.ds(0, half_pay), pl.ds(half_pay, tok_rows)
    s_z, s_x, s_c, s_t, s_g, s_f = (snd.at[j] for j in range(6))
    slots_copy = remote(
        blk.at[z, pl.ds(tok_rows, route), pl.ds(0, tok_rows)], tab, snd.at[9], one.at[1], {"pp": 0}
    )

    @pl.when(returns)
    def _():
        slots_copy.start()

    def z_at(i):
        away = (i + 1) // 2
        return (z + nz + jnp.where(i % 2 == 1, -away, away)) % nz

    def block_rows(zz, kind):
        lane = jnp.where(kind == 0, xl, 1 - xl)
        return pl.multiple_of((zz * 2 + lane) * cap, 16)

    def x_copy(i):
        zz = z_at(i)
        dst = xs.at[:, pl.ds(pl.multiple_of((zz * 2 + xl) * cap, 16), cap), pl.ds(mine_q, quarter)]
        return remote(stg.at[i], dst, s_x, xr.at[i], {"cp": cp_x})

    def share(i, kind):
        unit = kind * nz + i
        rows = pl.ds(block_rows(z_at(i), kind), cap)
        cols = pl.ds(mine_q, quarter)
        piece = xs.at[:, rows, cols]
        top, low = xs.at[0, rows, cols], xs.at[1, rows, cols]
        return (
            remote(piece, piece, s_c, cr.at[unit], {"dp": dp_c}),
            remote(top, top, s_t, yt.at[unit], {"dp": y_up}),
            remote(low, low, s_g, yg.at[unit], {"dp": y_dn}),
        )

    def from_y(i, kind):
        unit = kind * nz + i
        rows = pl.ds(block_rows(z_at(i), kind), cap)
        cols = pl.ds(other_q, quarter)
        piece = xs.at[:, rows, cols]
        top, low = xs.at[0, rows, cols], xs.at[1, rows, cols]
        return (
            remote(top, top, s_t, yt.at[unit], {"dp": y_up}),
            remote(low, low, s_g, yg.at[unit], {"dp": y_dn}),
            remote(piece, piece, s_f, cf.at[unit], {"dp": dp_c}),
        )

    def forward(i, kind):
        got_t, got_g, fwd = from_y(i, kind)
        got_t.wait_recv()
        got_g.wait_recv()
        fwd.start()

    def stage_block(i):
        zz = z_at(i)
        whole = blk.at[zz]

        @pl.when((i >= 1) & (i <= 6))
        def _():
            remote(whole, whole, s_z, zr.at[i], {"cp": z_up}).wait_recv()

        @pl.when(i == 7)
        def _():
            a, b = blk.at[zz, first, :], blk.at[zz, second, :]
            remote(a, a, s_z, zr.at[7], {"cp": z_up}).wait_recv()
            remote(b, b, s_z, zr.at[8], {"cp": z_dn}).wait_recv()

        @pl.when((i == 0) | (i == 1) | (i == 3))
        def _():
            remote(whole, whole, s_z, zr.at[jnp.where(i == 0, 1, i + 2)], {"cp": z_up}).start()

        @pl.when((i == 0) | (i == 2) | (i == 4))
        def _():
            remote(whole, whole, s_z, zr.at[i + 2], {"cp": z_dn}).start()

        @pl.when(i == 5)
        def _():
            a = blk.at[zz, first, :]
            remote(a, a, s_z, zr.at[7], {"cp": z_up}).start()

        @pl.when(i == 6)
        def _():
            b = blk.at[zz, second, :]
            remote(b, b, s_z, zr.at[8], {"cp": z_dn}).start()

        table = blk[zz, tok_rows:half_pay, 0 : 2 * tok_rows].astype(F32)
        slots, probs = table[:, :tok_rows], table[:, tok_rows:]
        c_iota = lax.broadcasted_iota(jnp.int32, (cap, tok_rows), 0).astype(F32)
        plain, scaled = [], []
        for expert in (cp, cp_x):
            sel = e_iota == expert
            s_row = jnp.sum(jnp.where(sel, slots, 0.0), axis=0, keepdims=True)
            p_row = jnp.sum(jnp.where(sel, probs, 0.0), axis=0, keepdims=True)
            hit = c_iota == s_row
            plain.append(jnp.where(hit, 1.0, 0.0).astype(BF16))
            scaled.append(jnp.where(hit, p_row, 0.0).astype(BF16))
        rows = pl.ds(block_rows(zz, 0), cap)
        cols = pl.ds(mine_q, quarter)
        for part, lo, onehots in ((0, 0, plain), (1, half_pay, scaled)):
            data = blk[zz, lo : lo + tok_rows, :]
            both = jnp.dot(
                jnp.concatenate(onehots, axis=0), data, preferred_element_type=F32
            ).astype(BF16)
            xs[part, rows, cols] = both[:cap]
            stg[i, part] = both[cap:]
        x_copy(i).start()
        for c in share(i, 0):
            c.start()

    by_feature = (((1,), (1,)), ((), ()))
    by_row = (((0,), (0,)), ((), ()))
    pair = 2 * cap

    chunk = width // ny
    half_w = chunk // 2

    def ccols(yy):
        return pl.ds(pl.multiple_of(yy * chunk, 128), chunk)

    def mine_of(i):
        return ipb.at[i, pl.ds(pl.multiple_of(core * cap, 16), cap)]

    def core_sum(i):
        src = ipb.at[i, pl.ds(pl.multiple_of((1 - core) * cap, 16), cap)]
        return remote(src, c1r.at[i], snd.at[6], c1m.at[i], {"dp": dp_c})

    def y_steps(i):
        up = i % 2 == 0
        fwd_y = jnp.where(up, (y + 1) % ny, (y + ny - 1) % ny)
        bwd_y = jnp.where(up, (y + ny - 1) % ny, (y + 1) % ny)
        fwd_to, bwd_to = {"dp": fwd_y * 2 + core}, {"dp": bwd_y * 2 + core}
        rows = pl.ds(pl.multiple_of(core * cap, 16), cap)
        s_y = snd.at[7]
        far = remote(
            ipb.at[i, rows, ccols((y + 2) % ny)], farr.at[i], s_y, fam.at[i], fwd_to
        )
        comb = remote(ipb.at[i, rows, ccols(fwd_y)], comr.at[i], s_y, com.at[i], fwd_to)
        direct = remote(ipb.at[i, rows, ccols(bwd_y)], dirr.at[i], s_y, dim.at[i], bwd_to)
        return far, comb, direct, fwd_y, rows

    def owner_copy(i, where):
        rows = pl.ds(pl.multiple_of(core * cap, 16), cap)
        return remote(ipb.at[i, rows, ccols(y)], l3r.at[z], snd.at[8], l3m.at[z], where)

    def proxy_copy(i):
        return remote(mine_of(i), mine_of(i), snd.at[10], pxm.at[i], proxy)

    def ret_a(i):
        core_sum(i).wait_recv()
        rows = pl.ds(pl.multiple_of(core * cap, 16), cap)
        ipb[i, rows, :] = (ipb[i, rows, :].astype(F32) + c1r[i].astype(F32)).astype(BF16)

        @pl.when(i < PROXIED)
        def _():
            proxy_copy(i).start()

        @pl.when(i >= PROXIED)
        def _():
            far, _, direct, _, _ = y_steps(i)
            far.start()
            direct.start()

    def proxy_a(i):
        proxy_copy(i).wait_recv()
        far, _, direct, _, _ = y_steps(i)
        far.start()
        direct.start()

    def ret_b(i):
        far, comb, _, fwd_y, rows = y_steps(i)
        far.wait_recv()
        cols = ccols(fwd_y)
        ipb[i, rows, cols] = (ipb[i, rows, cols].astype(F32) + farr[i].astype(F32)).astype(BF16)
        comb.start()

    def ret_c(i):
        _, comb, direct, _, rows = y_steps(i)
        comb.wait_recv()
        direct.wait_recv()
        total = ipb[i, rows, ccols(y)].astype(F32) + comr[i].astype(F32) + dirr[i].astype(F32)
        here = same & (i == 0) & jnp.logical_not(returns)

        @pl.when(here)
        def _():
            l3r[z] = total.astype(BF16)

        @pl.when(jnp.logical_not(here))
        def _():
            ipb[i, rows, ccols(y)] = total.astype(BF16)

            @pl.when(returns)
            def _():
                owner_copy(i, {"pp": 0, **owner(z_at(i))}).start()

            @pl.when(jnp.logical_not(returns))
            def _():
                owner_copy(i, owner(z_at(i))).start()

    def compute(i):
        zz = z_at(i)
        for kind in (0, 1):
            own, _, _ = share(i, kind)
            own.wait_recv()
            _, _, fwd = from_y(i, kind)
            fwd.wait_recv()
        rows = pl.ds(pl.multiple_of(zz * pair, 16), pair)
        x_rows = xs[0, rows, :]
        gate_pre = lax.dot_general(x_rows, wg[...], by_feature, preferred_element_type=F32)
        up_pre = lax.dot_general(x_rows, wu[...], by_feature, preferred_element_type=F32)
        g_hid = lax.dot_general(xs[1, rows, :], wd[...], by_feature, preferred_element_type=F32)
        sigma = jax.nn.sigmoid(gate_pre)
        silu = gate_pre * sigma
        hidden = (silu * up_pre).astype(BF16)
        hid[rows, :] = hidden
        prod = hidden.astype(F32) * g_hid
        high = prod.astype(BF16)
        low = (prod - high.astype(F32)).astype(BF16)
        ones = jnp.ones((8, prod.shape[1]), BF16)
        for k in (0, 1):
            part = slice(k * cap, (k + 1) * cap)
            sums = lax.dot_general(ones, high[part], by_feature, preferred_element_type=F32)
            sums += lax.dot_general(ones, low[part], by_feature, preferred_element_type=F32)
            ptab[0, zz * 2 + k, :, 0:cap] = sums
        g_gate = (g_hid * up_pre * sigma * (1.0 + gate_pre * (1.0 - sigma))).astype(BF16)
        g_up = (g_hid * silu).astype(BF16)
        ggp[rows, :] = g_gate
        gup[rows, :] = g_up

        @pl.when(returns)
        def _():
            step = 512
            for lo in range(0, width, step):
                part = jnp.dot(g_gate, wg[:, lo : lo + step], preferred_element_type=F32)
                part += jnp.dot(g_up, wu[:, lo : lo + step], preferred_element_type=F32)
                ipb[i, :, lo : lo + step] = part.astype(BF16)
            core_sum(i).start()

    def pair_copy(r):
        to = (dp_c, (y + 1 - 2 * (y % 2)) * 2 + core, (ny - 1 - y) * 2 + core)[r]
        return remote(ptab.at[r], prcv.at[r], psn.at[r], ppm.at[r], {"dp": to})

    def pair_sum(r):
        pair_copy(r).wait_recv()
        ptab[r + 1] = ptab[r] + prcv[r]

    def prob_copy(dz):
        zz = (z + dz) % nz
        return remote(
            ptab.at[3, zz * 2 + core], pcol.at[z], psn.at[3], pcm.at[z], owner(zz)
        )

    def prob_spread():
        for dz in range(1, nz):
            prob_copy(dz).start()

        @pl.when(jnp.logical_not(same))
        def _():
            prob_copy(0).start()

        @pl.when(same)
        def _():
            pcol[z] = ptab[3, z * 2 + core]

    def own_hits(table, expert):
        row = jnp.sum(jnp.where(e_iota == expert, table, 0.0), axis=0, keepdims=True)
        c_iota = lax.broadcasted_iota(jnp.int32, (cap, tok_rows), 0).astype(F32)
        return jnp.where(c_iota == row, 1.0, 0.0).astype(BF16)

    def each_source(ref, sems, sem):
        for dz in range(1, nz):
            src = (z + dz) % nz
            remote(ref.at[src], ref.at[src], sem, sems.at[src], owner(z)).wait_recv()

        @pl.when(jnp.logical_not(same))
        def _():
            remote(ref.at[z], ref.at[z], sem, sems.at[z], owner(z)).wait_recv()

    last_copy = remote(pfin.at[0], pfin.at[1], psn.at[4], one.at[0], {"dp": dp_c})

    def prob_pick():
        each_source(pcol, pcm, psn.at[3])
        acc = jnp.zeros(id_val.shape, F32)
        table = blk[z, tok_rows:half_pay, 0:tok_rows].astype(F32)
        for zz in range(nz):
            val = pcol[zz][:, 0:cap]
            high = val.astype(BF16)
            low = (val - high.astype(F32)).astype(BF16)
            hits = own_hits(table, zz * 2 + core)
            got = jnp.dot(high, hits, preferred_element_type=F32)
            got += jnp.dot(low, hits, preferred_element_type=F32)
            acc = jnp.where(ids[...] == zz * 2 + core, got, acc)
        pfin[0] = acc
        last_copy.start()

    grad_step = 512
    n_grad = width // grad_step

    def grads(t):
        cols = pl.ds(pl.multiple_of(t * grad_step, 128), grad_step)
        x_cols = xs[0, :, cols]
        grb[0, :, cols] = lax.dot_general(
            ggp[...], x_cols, by_row, preferred_element_type=F32
        ).astype(BF16)
        grb[1, :, cols] = lax.dot_general(
            gup[...], x_cols, by_row, preferred_element_type=F32
        ).astype(BF16)
        grb[2, :, cols] = lax.dot_general(
            hid[...], xs[1, :, cols], by_row, preferred_element_type=F32
        ).astype(BF16)

    def step_fn(i, carry):
        @pl.when(i < nz)
        def _():
            stage_block(i)

        @pl.when((i >= 1) & (i < nz + 1))
        def _():
            x_copy(i - 1).wait_recv()
            for c in share(i - 1, 1):
                c.start()

        @pl.when((i >= 2) & (i < nz + 2))
        def _():
            forward(i - 2, 0)

        @pl.when((i >= 3) & (i < nz + 3))
        def _():
            forward(i - 3, 1)

        @pl.when(i == 4)
        def _():
            for c in weights:
                c.wait()

        for lag, low, stage in ((9, PROXIED, ret_c), (7, PROXIED, ret_b), (5, 0, ret_a)):

            @pl.when(returns & (i >= lag + low) & (i < nz + lag))
            def _(lag=lag, stage=stage):
                stage(i - lag)

        for lag, stage in ((14, ret_c), (12, ret_b), (10, proxy_a)):

            @pl.when(jnp.logical_not(returns) & (i >= lag) & (i < 2 * PROXIED + lag) & (i % 2 == 0))
            def _(lag=lag, stage=stage):
                stage((i - lag) // 2)

        @pl.when((i >= 4) & (i < nz + 4))
        def _():
            compute(i - 4)

        first_free = nz + 4

        @pl.when(i == first_free)
        def _():
            pair_copy(0).start()

        for r in (0, 1):

            @pl.when(i == first_free + 1 + r)
            def _(r=r):
                pair_sum(r)
                pair_copy(r + 1).start()

        @pl.when(i == first_free + 3)
        def _():
            pair_sum(2)
            prob_spread()

        @pl.when(i == first_free + 5)
        def _():
            prob_pick()

        @pl.when(i >= first_free)
        def _():
            grads(i - first_free)

        return carry

    lax.fori_loop(0, nz + 4 + n_grad, step_fn, 0)

    outs = [
        pltpu.make_async_copy(grb.at[j], o, loc.at[j]) for j, o in enumerate((gg_out, ug_out, dg_out))
    ]
    for c in outs:
        c.start()
    swap = remote(fxs, fxr, snd.at[11], one.at[2], {"dp": dp_c})

    @pl.when(returns)
    def _():
        passed_out[...] = jnp.zeros_like(passed_out)

    @pl.when(jnp.logical_not(returns))
    def _():
        slots_copy.wait_recv()
        table = tab[...].astype(F32)
        hits, rows = [], []
        for i in range(nz):
            away = (i + 1) // 2
            src = (z + nz + (away if i % 2 == 1 else -away)) % nz
            landed = remote(l3r.at[src], l3r.at[src], snd.at[8], l3m.at[src], owner(z))
            if i == 0:
                pl.when(jnp.logical_not(same))(landed.wait_recv)
            else:
                landed.wait_recv()
            hits.append(own_hits(table, src * 2 + (1 - core if i < PROXIED else core)))
            rows.append(l3r[src])
        tot = lax.dot_general(
            jnp.concatenate(hits, axis=0), jnp.concatenate(rows, axis=0), by_row,
            preferred_element_type=F32,
        ).T

        @pl.when(core == 0)
        def _():
            fxs[...] = tot[half_w:]

        @pl.when(core == 1)
        def _():
            fxs[...] = tot[:half_w]

        swap.start()
        kept = jnp.where(core == 0, tot[:half_w], tot[half_w:])
        swap.wait_recv()
        passed_out[...] = (kept + fxr[...]).astype(BF16)

    last_copy.wait_recv()
    prob_out[...] = (pfin[0] + pfin[1]) / prb[...].astype(F32)
    cols, ocols = pl.ds(mine_q, quarter), pl.ds(other_q, quarter)
    seven = blk.at[pl.ds(0, nz - 1)]
    remote(seven, seven, s_z, zr.at[0], {"cp": z_up}).wait_send()
    remote(stg, stg, s_x, zr.at[0], {"cp": cp_x}).wait_send()
    a = xs.at[:, :, cols]
    remote(a, a, s_c, zr.at[0], {"dp": dp_c}).wait_send()
    a = xs.at[0, :, cols]
    remote(a, a, s_t, zr.at[0], {"dp": y_up}).wait_send()
    a = xs.at[1, :, cols]
    remote(a, a, s_g, zr.at[0], {"dp": y_dn}).wait_send()
    a = xs.at[:, :, ocols]
    remote(a, a, s_f, zr.at[0], {"dp": dp_c}).wait_send()
    for r in (0, 1, 2):
        pair_copy(r).wait_send()
    last_copy.wait_send()
    seven_p = pcol.at[pl.ds(0, nz - 1)]

    @pl.when(same)
    def _():
        remote(seven_p, seven_p, psn.at[3], one.at[0], owner(z)).wait_send()

    @pl.when(jnp.logical_not(same))
    def _():
        remote(pcol, pcol, psn.at[3], one.at[0], owner(z)).wait_send()

    def sent_pieces(pieces, sem):
        ref = dirr.at[pl.ds(0, pieces)]
        remote(ref, ref, sem, one.at[0], {"dp": y_up}).wait_send()

    @pl.when(returns)
    def _():
        remote(c1r, c1r, snd.at[6], one.at[0], {"dp": dp_c}).wait_send()
        ref = c1r.at[pl.ds(0, PROXIED)]
        remote(ref, ref, snd.at[10], one.at[0], proxy).wait_send()
        many = ipb.at[pl.ds(0, nz - PROXIED), pl.ds(0, cap), pl.ds(0, 3 * chunk)]
        remote(many, many, snd.at[7], one.at[0], {"dp": y_up}).wait_send()
        sent_pieces(nz - PROXIED, snd.at[8])
        slots_copy.wait_send()

    @pl.when(jnp.logical_not(returns))
    def _():
        many = ipb.at[pl.ds(0, PROXIED), pl.ds(0, cap), pl.ds(0, 3 * chunk)]
        remote(many, many, snd.at[7], one.at[0], {"dp": y_up}).wait_send()
        swap.wait_send()

    @pl.when(jnp.logical_not(returns) & same)
    def _():
        sent_pieces(PROXIED - 1, snd.at[8])

    @pl.when(jnp.logical_not(returns) & jnp.logical_not(same))
    def _():
        sent_pieces(PROXIED, snd.at[8])

    for c in outs:
        c.wait()


def expert_call(tokens, out_grad, ids_t, probs_t, w_gate, w_up, w_down):
    tok_rows, width = tokens.shape
    experts = lax.axis_size("cp")
    nz, ny = experts // 2, lax.axis_size("dp") // 2
    top = ids_t.shape[0]
    cap = tok_rows * top * CAP_NUM // (CAP_DEN * experts)
    ff = w_gate.shape[0]
    rows = experts * cap
    quarter = width // 4
    pay = 2 * tok_rows + 16
    anyspace = pl.BlockSpec(memory_space=pl.ANY)
    vmem = pl.BlockSpec(memory_space=pltpu.VMEM)
    wshape = jax.ShapeDtypeStruct((ff, width), BF16)
    dma = pltpu.SemaphoreType.DMA
    return pl.pallas_call(
        functools.partial(expert_kernel, (tok_rows, width, experts, cap, nz, ny)),
        out_shape=(
            jax.ShapeDtypeStruct((width // (2 * ny), tok_rows), BF16),
            jax.ShapeDtypeStruct((top, tok_rows), F32),
            wshape, wshape, wshape,
        ),
        in_specs=[anyspace, anyspace, vmem, vmem, anyspace, anyspace, anyspace],
        out_specs=(vmem, vmem, anyspace, anyspace, anyspace),
        scratch_shapes=[
            pltpu.VMEM((nz, pay, quarter), BF16),
            pltpu.VMEM((nz, 2, cap, quarter), BF16),
            pltpu.VMEM((2, rows, width), BF16),
            pltpu.VMEM((ff, width), BF16),
            pltpu.VMEM((ff, width), BF16),
            pltpu.VMEM((ff, width), BF16),
            pltpu.VMEM((rows, ff), BF16),
            pltpu.VMEM((rows, ff), BF16),
            pltpu.VMEM((rows, ff), BF16),
            pltpu.VMEM((3, ff, width), BF16),
            pltpu.VMEM((nz, 2 * cap, width), BF16),
            pltpu.VMEM((nz, cap, width), BF16),
            pltpu.VMEM((nz, cap, width // ny), BF16),
            pltpu.VMEM((nz, cap, width // ny), BF16),
            pltpu.VMEM((nz, cap, width // ny), BF16),
            pltpu.VMEM((nz, cap, width // ny), BF16),
            pltpu.VMEM((4, experts, 8, 128), F32),
            pltpu.VMEM((3, experts, 8, 128), F32),
            pltpu.VMEM((nz, 8, 128), F32),
            pltpu.VMEM((2, top, tok_rows), F32),
            pltpu.VMEM((width // (2 * ny), tok_rows), F32),
            pltpu.VMEM((width // (2 * ny), tok_rows), F32),
            pltpu.VMEM((16, tok_rows), BF16),
            dma((5,)), dma((9,)), dma((nz,)), dma((2 * nz,)), dma((2 * nz,)), dma((2 * nz,)),
            dma((2 * nz,)), dma((12,)), dma((nz,)), dma((nz,)), dma((nz,)), dma((nz,)), dma((nz,)),
            dma((PROXIED,)), dma((3,)), dma((nz,)), dma((5,)), dma((3,)),
        ],
        compiler_params=pltpu.CompilerParams(
            collective_id=0, has_side_effects=True, vmem_limit_bytes=60 * 1024 * 1024
        ),
        name="expert",
    )(tokens, out_grad, ids_t, probs_t, w_gate, w_up, w_down)


def body(tokens, out_grad, probs, expert_ids, w_gate, w_up, w_down):
    passed, prob_grad, gate_grad, up_grad, down_grad = expert_call(
        tokens[0], out_grad[0], expert_ids[0].T, probs[0].T, w_gate[0, 0], w_up[0, 0], w_down[0, 0]
    )
    return (
        passed.T[None],
        prob_grad.T[None],
        gate_grad[None, None],
        up_grad[None, None],
        down_grad[None, None],
    )


def solution(mesh):
    in_specs = (
        P("pp", "cp", None),
        P("pp", "cp", None),
        P("pp", "cp", None),
        P("pp", "cp", None),
        P("pp", "cp", "dp", None),
        P("pp", "cp", "dp", None),
        P("pp", "cp", "dp", None),
    )
    out_specs = (
        P("pp", "cp", "dp"),
        P("pp", "cp", None),
        P("pp", "cp", "dp", None),
        P("pp", "cp", "dp", None),
        P("pp", "cp", "dp", None),
    )
    return jax.shard_map(body, mesh=mesh, in_specs=in_specs, out_specs=out_specs, check_vma=False)
```

```python
import functools
import jax
import jax.numpy as jnp
from jax import lax
from jax.experimental import pallas as pl
from jax.experimental.pallas import tpu as pltpu
from jax.sharding import PartitionSpec as P

CAP_NUM, CAP_DEN = 5, 4
MESH = pl.DeviceIdType.MESH
PROXIED = 3
F32, BF16 = jnp.float32, jnp.bfloat16


def expert_kernel(
    dims, tok, grd, ids, prb, w_gate, w_up, w_down,
    passed_out, prob_out, gg_out, ug_out, dg_out,
    blk, stg, xs, wg, wu, wd, hid, ggp, gup, ipb, c1r, farr, comr, dirr, l3r,
    ptab, pcol, pall, fxs, fxr, tab,
    loc, zr, xr, cr, yt, yg, cf, snd, c1m, fam, com, dim, l3m, pxm, pcm, pam, psn, one,
):
    tok_rows, width, experts, cap, nz, ny = dims
    quarter = width // 4
    route = 16
    pay = 2 * tok_rows + route
    half_pay = tok_rows + route
    dp = lax.axis_index("dp")
    cp = lax.axis_index("cp")
    ndp, ncp = 2 * ny, 2 * nz
    z, xl = cp // 2, cp % 2
    y, core = dp // 2, dp % 2
    half = y % 2
    mine_q = pl.multiple_of((half * 2 + core) * quarter, 128)
    other_q = pl.multiple_of(((1 - half) * 2 + core) * quarter, 128)
    cp_x = z * 2 + (1 - xl)
    dp_c = y * 2 + (1 - core)
    z_up = ((z + 1) % nz) * 2 + xl
    z_dn = ((z + nz - 1) % nz) * 2 + xl
    y_up = ((y + 1) % ny) * 2 + core
    y_dn = ((y + ny - 1) % ny) * 2 + core

    pp = lax.axis_index("pp")
    returns = pp == 1
    same = core == xl
    owner_dp = y * 2 + xl

    def owner(zz):
        return {"cp": zz * 2 + core, "dp": owner_dp}

    def other_owner(zz):
        return {"pp": 1 - pp, "cp": zz * 2 + core, "dp": owner_dp}

    proxy = {"pp": 1 - pp, "cp": cp_x}

    barrier = pltpu.get_barrier_semaphore()

    def greet(where):
        pl.semaphore_signal(barrier, inc=1, device_id=where, device_id_type=MESH)

    for d in range(1, ncp):
        greet({"cp": (cp + d) % ncp})
    for d in range(1, ndp):
        greet({"dp": (dp + d) % ndp})
    greet({"pp": 1 - pp})
    greet(proxy)
    for zz in range(nz):
        greet(other_owner(zz))

    @pl.when(jnp.logical_not(same))
    def _():
        for zz in range(nz):
            greet(owner(zz))

    loads = [
        pltpu.make_async_copy(
            tok.at[:, pl.ds(mine_q, quarter)], blk.at[z, pl.ds(0, tok_rows), :], loc.at[0]
        ),
        pltpu.make_async_copy(
            grd.at[:, pl.ds(mine_q, quarter)], blk.at[z, pl.ds(half_pay, tok_rows), :], loc.at[1]
        ),
    ]
    weights = [
        pltpu.make_async_copy(w_gate, wg, loc.at[2]),
        pltpu.make_async_copy(w_up, wu, loc.at[3]),
        pltpu.make_async_copy(w_down, wd, loc.at[4]),
    ]
    for c in loads:
        c.start()
    for c in weights:
        c.start()

    e_iota = lax.broadcasted_iota(jnp.int32, (experts, tok_rows), 0)
    has = jnp.zeros((experts, tok_rows), F32)
    wgt = jnp.zeros((experts, tok_rows), F32)
    id_val = ids[...]
    prb_val = prb[...].astype(F32)
    for k in range(id_val.shape[0]):
        hit = id_val[k : k + 1, :] == e_iota
        has = jnp.where(hit, 1.0, has)
        wgt = jnp.where(hit, prb_val[k : k + 1, :], wgt)
    earlier = (
        lax.broadcasted_iota(jnp.int32, (tok_rows, tok_rows), 0)
        < lax.broadcasted_iota(jnp.int32, (tok_rows, tok_rows), 1)
    )
    slot = jnp.dot(
        has.astype(BF16), jnp.where(earlier, 1.0, 0.0).astype(BF16), preferred_element_type=F32
    )
    slot = jnp.where(has > 0.0, slot, -1.0)
    blk[z, tok_rows:half_pay, :] = jnp.zeros((route, quarter), BF16)
    blk[z, tok_rows:half_pay, 0:tok_rows] = slot.astype(BF16)
    blk[z, tok_rows:half_pay, tok_rows : 2 * tok_rows] = wgt.astype(BF16)
    for c in loads:
        c.wait()
    ptab[...] = jnp.zeros_like(ptab)
    pl.semaphore_wait(barrier, ncp + ndp + nz + jnp.where(same, 0, nz))

    def remote(src, dst, s, r, where):
        return pltpu.make_async_remote_copy(
            src_ref=src, dst_ref=dst, send_sem=s, recv_sem=r, device_id=where, device_id_type=MESH
        )

    first, second = pl.ds(0, half_pay), pl.ds(half_pay, tok_rows)
    s_z, s_x, s_c, s_t, s_g, s_f = (snd.at[j] for j in range(6))
    slots_copy = remote(
        blk.at[z, pl.ds(tok_rows, route), pl.ds(0, tok_rows)], tab, snd.at[9], one.at[1], {"pp": 0}
    )

    @pl.when(returns)
    def _():
        slots_copy.start()

    def z_at(i):
        away = (i + 1) // 2
        return (z + nz + jnp.where(i % 2 == 1, -away, away)) % nz

    def block_rows(zz, kind):
        lane = jnp.where(kind == 0, xl, 1 - xl)
        return pl.multiple_of((zz * 2 + lane) * cap, 16)

    def x_copy(i):
        zz = z_at(i)
        dst = xs.at[:, pl.ds(pl.multiple_of((zz * 2 + xl) * cap, 16), cap), pl.ds(mine_q, quarter)]
        return remote(stg.at[i], dst, s_x, xr.at[i], {"cp": cp_x})

    def share(i, kind):
        unit = kind * nz + i
        rows = pl.ds(block_rows(z_at(i), kind), cap)
        cols = pl.ds(mine_q, quarter)
        piece = xs.at[:, rows, cols]
        top, low = xs.at[0, rows, cols], xs.at[1, rows, cols]
        return (
            remote(piece, piece, s_c, cr.at[unit], {"dp": dp_c}),
            remote(top, top, s_t, yt.at[unit], {"dp": y_up}),
            remote(low, low, s_g, yg.at[unit], {"dp": y_dn}),
        )

    def from_y(i, kind):
        unit = kind * nz + i
        rows = pl.ds(block_rows(z_at(i), kind), cap)
        cols = pl.ds(other_q, quarter)
        piece = xs.at[:, rows, cols]
        top, low = xs.at[0, rows, cols], xs.at[1, rows, cols]
        return (
            remote(top, top, s_t, yt.at[unit], {"dp": y_up}),
            remote(low, low, s_g, yg.at[unit], {"dp": y_dn}),
            remote(piece, piece, s_f, cf.at[unit], {"dp": dp_c}),
        )

    def forward(i, kind):
        got_t, got_g, fwd = from_y(i, kind)
        got_t.wait_recv()
        got_g.wait_recv()
        fwd.start()

    def stage_block(i):
        zz = z_at(i)
        whole = blk.at[zz]

        @pl.when((i >= 1) & (i <= 6))
        def _():
            remote(whole, whole, s_z, zr.at[i], {"cp": z_up}).wait_recv()

        @pl.when(i == 7)
        def _():
            a, b = blk.at[zz, first, :], blk.at[zz, second, :]
            remote(a, a, s_z, zr.at[7], {"cp": z_up}).wait_recv()
            remote(b, b, s_z, zr.at[8], {"cp": z_dn}).wait_recv()

        @pl.when((i == 0) | (i == 1) | (i == 3))
        def _():
            remote(whole, whole, s_z, zr.at[jnp.where(i == 0, 1, i + 2)], {"cp": z_up}).start()

        @pl.when((i == 0) | (i == 2) | (i == 4))
        def _():
            remote(whole, whole, s_z, zr.at[i + 2], {"cp": z_dn}).start()

        @pl.when(i == 5)
        def _():
            a = blk.at[zz, first, :]
            remote(a, a, s_z, zr.at[7], {"cp": z_up}).start()

        @pl.when(i == 6)
        def _():
            b = blk.at[zz, second, :]
            remote(b, b, s_z, zr.at[8], {"cp": z_dn}).start()

        table = blk[zz, tok_rows:half_pay, 0 : 2 * tok_rows].astype(F32)
        slots, probs = table[:, :tok_rows], table[:, tok_rows:]
        c_iota = lax.broadcasted_iota(jnp.int32, (cap, tok_rows), 0).astype(F32)
        plain, scaled = [], []
        for expert in (cp, cp_x):
            sel = e_iota == expert
            s_row = jnp.sum(jnp.where(sel, slots, 0.0), axis=0, keepdims=True)
            p_row = jnp.sum(jnp.where(sel, probs, 0.0), axis=0, keepdims=True)
            hit = c_iota == s_row
            plain.append(jnp.where(hit, 1.0, 0.0).astype(BF16))
            scaled.append(jnp.where(hit, p_row, 0.0).astype(BF16))
        rows = pl.ds(block_rows(zz, 0), cap)
        cols = pl.ds(mine_q, quarter)
        for part, lo, onehots in ((0, 0, plain), (1, half_pay, scaled)):
            data = blk[zz, lo : lo + tok_rows, :]
            both = jnp.dot(
                jnp.concatenate(onehots, axis=0), data, preferred_element_type=F32
            ).astype(BF16)
            xs[part, rows, cols] = both[:cap]
            stg[i, part] = both[cap:]
        x_copy(i).start()
        for c in share(i, 0):
            c.start()

    by_feature = (((1,), (1,)), ((), ()))
    by_row = (((0,), (0,)), ((), ()))
    pair = 2 * cap

    chunk = width // ny
    half_w = chunk // 2

    def ccols(yy):
        return pl.ds(pl.multiple_of(yy * chunk, 128), chunk)

    def mine_of(i):
        return ipb.at[i, pl.ds(pl.multiple_of(core * cap, 16), cap)]

    def core_sum(i):
        src = ipb.at[i, pl.ds(pl.multiple_of((1 - core) * cap, 16), cap)]
        return remote(src, c1r.at[i], snd.at[6], c1m.at[i], {"dp": dp_c})

    def y_steps(i):
        up = i % 2 == 0
        fwd_y = jnp.where(up, (y + 1) % ny, (y + ny - 1) % ny)
        bwd_y = jnp.where(up, (y + ny - 1) % ny, (y + 1) % ny)
        fwd_to, bwd_to = {"dp": fwd_y * 2 + core}, {"dp": bwd_y * 2 + core}
        rows = pl.ds(pl.multiple_of(core * cap, 16), cap)
        s_y = snd.at[7]
        far = remote(
            ipb.at[i, rows, ccols((y + 2) % ny)], farr.at[i], s_y, fam.at[i], fwd_to
        )
        comb = remote(ipb.at[i, rows, ccols(fwd_y)], comr.at[i], s_y, com.at[i], fwd_to)
        direct = remote(ipb.at[i, rows, ccols(bwd_y)], dirr.at[i], s_y, dim.at[i], bwd_to)
        return far, comb, direct, fwd_y, rows

    def owner_copy(i, where):
        rows = pl.ds(pl.multiple_of(core * cap, 16), cap)
        return remote(ipb.at[i, rows, ccols(y)], l3r.at[z], snd.at[8], l3m.at[z], where)

    def proxy_copy(i):
        return remote(mine_of(i), mine_of(i), snd.at[10], pxm.at[i], proxy)

    def ret_a(i):
        core_sum(i).wait_recv()
        rows = pl.ds(pl.multiple_of(core * cap, 16), cap)
        ipb[i, rows, :] = (ipb[i, rows, :].astype(F32) + c1r[i].astype(F32)).astype(BF16)

        @pl.when(i < PROXIED)
        def _():
            proxy_copy(i).start()

        @pl.when(i >= PROXIED)
        def _():
            far, _, direct, _, _ = y_steps(i)
            far.start()
            direct.start()

    def proxy_a(i):
        proxy_copy(i).wait_recv()
        far, _, direct, _, _ = y_steps(i)
        far.start()
        direct.start()

    def ret_b(i):
        far, comb, _, fwd_y, rows = y_steps(i)
        far.wait_recv()
        cols = ccols(fwd_y)
        ipb[i, rows, cols] = (ipb[i, rows, cols].astype(F32) + farr[i].astype(F32)).astype(BF16)
        comb.start()

    def ret_c(i):
        _, comb, direct, _, rows = y_steps(i)
        comb.wait_recv()
        direct.wait_recv()
        total = ipb[i, rows, ccols(y)].astype(F32) + comr[i].astype(F32) + dirr[i].astype(F32)
        here = same & (i == 0) & jnp.logical_not(returns)

        @pl.when(here)
        def _():
            l3r[z] = total.astype(BF16)

        @pl.when(jnp.logical_not(here))
        def _():
            ipb[i, rows, ccols(y)] = total.astype(BF16)

            @pl.when(returns)
            def _():
                owner_copy(i, {"pp": 0, **owner(z_at(i))}).start()

            @pl.when(jnp.logical_not(returns))
            def _():
                owner_copy(i, owner(z_at(i))).start()

    def prob_send(i, k):
        zz = z_at(i)
        here = (i == 0) & (xl == k)

        @pl.when(here)
        def _():
            pcol[cp] = ptab[cp]

        @pl.when(jnp.logical_not(here))
        def _():
            remote(
                ptab.at[zz * 2 + k], pcol.at[cp], psn.at[0], pcm.at[cp], {"cp": zz * 2 + k}
            ).start()

    def compute(i):
        zz = z_at(i)
        for kind in (0, 1):
            own, _, _ = share(i, kind)
            own.wait_recv()
            _, _, fwd = from_y(i, kind)
            fwd.wait_recv()
        rows = pl.ds(pl.multiple_of(zz * pair, 16), pair)
        x_rows = xs[0, rows, :]
        gate_pre = lax.dot_general(x_rows, wg[...], by_feature, preferred_element_type=F32)
        up_pre = lax.dot_general(x_rows, wu[...], by_feature, preferred_element_type=F32)
        g_hid = lax.dot_general(xs[1, rows, :], wd[...], by_feature, preferred_element_type=F32)
        sigma = jax.nn.sigmoid(gate_pre)
        silu = gate_pre * sigma
        hidden = (silu * up_pre).astype(BF16)
        hid[rows, :] = hidden
        prod = hidden.astype(F32) * g_hid
        high = prod.astype(BF16)
        low = (prod - high.astype(F32)).astype(BF16)
        ones = jnp.ones((8, prod.shape[1]), BF16)
        for k in (0, 1):
            part = slice(k * cap, (k + 1) * cap)
            sums = lax.dot_general(ones, high[part], by_feature, preferred_element_type=F32)
            sums += lax.dot_general(ones, low[part], by_feature, preferred_element_type=F32)
            ptab[zz * 2 + k, :, 0:cap] = sums
            prob_send(i, k)
        g_gate = (g_hid * up_pre * sigma * (1.0 + gate_pre * (1.0 - sigma))).astype(BF16)
        g_up = (g_hid * silu).astype(BF16)
        ggp[rows, :] = g_gate
        gup[rows, :] = g_up

        @pl.when(returns)
        def _():
            step = 512
            for lo in range(0, width, step):
                part = jnp.dot(g_gate, wg[:, lo : lo + step], preferred_element_type=F32)
                part += jnp.dot(g_up, wu[:, lo : lo + step], preferred_element_type=F32)
                ipb[i, :, lo : lo + step] = part.astype(BF16)
            core_sum(i).start()

    def own_hits(table, expert):
        row = jnp.sum(jnp.where(e_iota == expert, table, 0.0), axis=0, keepdims=True)
        c_iota = lax.broadcasted_iota(jnp.int32, (cap, tok_rows), 0).astype(F32)
        return jnp.where(c_iota == row, 1.0, 0.0).astype(BF16)

    def dp_copy(d):
        return remote(
            pall.at[dp], pall.at[dp], psn.at[1], pam.at[dp], {"dp": (dp + d) % ndp}
        )

    def prob_pick():
        for d in range(1, ncp):
            src = (cp + d) % ncp
            remote(
                pcol.at[src], pcol.at[src], psn.at[0], pcm.at[src], {"cp": src}
            ).wait_recv()
        acc = jnp.zeros(id_val.shape, F32)
        table = blk[z, tok_rows:half_pay, 0:tok_rows].astype(F32)
        for expert in range(experts):
            val = pcol[expert][:, 0:cap]
            high = val.astype(BF16)
            low = (val - high.astype(F32)).astype(BF16)
            hits = own_hits(table, expert)
            got = jnp.dot(high, hits, preferred_element_type=F32)
            got += jnp.dot(low, hits, preferred_element_type=F32)
            acc = jnp.where(ids[...] == expert, got, acc)
        pall[dp] = acc
        for d in range(1, ndp):
            dp_copy(d).start()

    def prob_finish():
        total = pall[dp]
        for d in range(1, ndp):
            src = (dp + d) % ndp
            remote(
                pall.at[src], pall.at[src], psn.at[1], pam.at[src], {"dp": src}
            ).wait_recv()
            total += pall[src]
        prob_out[...] = total / prb[...].astype(F32)

    grad_step = 512
    n_grad = width // grad_step

    def grads(t):
        cols = pl.ds(pl.multiple_of(t * grad_step, 128), grad_step)
        x_cols = xs[0, :, cols]
        gg_out[:, cols] = lax.dot_general(
            ggp[...], x_cols, by_row, preferred_element_type=F32
        ).astype(BF16)
        ug_out[:, cols] = lax.dot_general(
            gup[...], x_cols, by_row, preferred_element_type=F32
        ).astype(BF16)
        dg_out[:, cols] = lax.dot_general(
            hid[...], xs[1, :, cols], by_row, preferred_element_type=F32
        ).astype(BF16)

    def step_fn(i, carry):
        @pl.when(i < nz)
        def _():
            stage_block(i)

        @pl.when((i >= 1) & (i < nz + 1))
        def _():
            x_copy(i - 1).wait_recv()
            for c in share(i - 1, 1):
                c.start()

        @pl.when((i >= 2) & (i < nz + 2))
        def _():
            forward(i - 2, 0)

        @pl.when((i >= 3) & (i < nz + 3))
        def _():
            forward(i - 3, 1)

        @pl.when(i == 4)
        def _():
            for c in weights:
                c.wait()

        for lag, low, stage in ((9, PROXIED, ret_c), (7, PROXIED, ret_b), (5, 0, ret_a)):

            @pl.when(returns & (i >= lag + low) & (i < nz + lag))
            def _(lag=lag, stage=stage):
                stage(i - lag)

        for lag, stage in ((14, ret_c), (12, ret_b), (10, proxy_a)):

            @pl.when(jnp.logical_not(returns) & (i >= lag) & (i < 2 * PROXIED + lag) & (i % 2 == 0))
            def _(lag=lag, stage=stage):
                stage((i - lag) // 2)

        @pl.when((i >= 4) & (i < nz + 4))
        def _():
            compute(i - 4)

        first_free = nz + 4

        @pl.when(i == first_free + 4)
        def _():
            prob_pick()

        @pl.when(i >= first_free)
        def _():
            grads(i - first_free)

        return carry

    lax.fori_loop(0, nz + 4 + n_grad, step_fn, 0)

    swap = remote(fxs, fxr, snd.at[11], one.at[2], {"dp": dp_c})

    @pl.when(returns)
    def _():
        passed_out[...] = jnp.zeros_like(passed_out)

    @pl.when(jnp.logical_not(returns))
    def _():
        slots_copy.wait_recv()
        table = tab[...].astype(F32)
        hits, rows = [], []
        for i in range(nz):
            away = (i + 1) // 2
            src = (z + nz + (away if i % 2 == 1 else -away)) % nz
            landed = remote(l3r.at[src], l3r.at[src], snd.at[8], l3m.at[src], owner(z))
            if i == 0:
                pl.when(jnp.logical_not(same))(landed.wait_recv)
            else:
                landed.wait_recv()
            hits.append(own_hits(table, src * 2 + (1 - core if i < PROXIED else core)))
            rows.append(l3r[src])
        tot = lax.dot_general(
            jnp.concatenate(hits, axis=0), jnp.concatenate(rows, axis=0), by_row,
            preferred_element_type=F32,
        ).T

        @pl.when(core == 0)
        def _():
            fxs[...] = tot[half_w:]

        @pl.when(core == 1)
        def _():
            fxs[...] = tot[:half_w]

        swap.start()
        kept = jnp.where(core == 0, tot[:half_w], tot[half_w:])
        swap.wait_recv()
        passed_out[...] = (kept + fxr[...]).astype(BF16)

    prob_finish()
    cols, ocols = pl.ds(mine_q, quarter), pl.ds(other_q, quarter)
    seven = blk.at[pl.ds(0, nz - 1)]
    remote(seven, seven, s_z, zr.at[0], {"cp": z_up}).wait_send()
    remote(stg, stg, s_x, zr.at[0], {"cp": cp_x}).wait_send()
    a = xs.at[:, :, cols]
    remote(a, a, s_c, zr.at[0], {"dp": dp_c}).wait_send()
    a = xs.at[0, :, cols]
    remote(a, a, s_t, zr.at[0], {"dp": y_up}).wait_send()
    a = xs.at[1, :, cols]
    remote(a, a, s_g, zr.at[0], {"dp": y_dn}).wait_send()
    a = xs.at[:, :, ocols]
    remote(a, a, s_f, zr.at[0], {"dp": dp_c}).wait_send()
    most = pcol.at[pl.ds(0, experts - 1)]
    remote(most, most, psn.at[0], one.at[0], {"cp": z_up}).wait_send()
    most = pall.at[pl.ds(0, ndp - 1)]
    remote(most, most, psn.at[1], one.at[0], {"dp": y_up}).wait_send()

    def sent_pieces(pieces, sem):
        ref = dirr.at[pl.ds(0, pieces)]
        remote(ref, ref, sem, one.at[0], {"dp": y_up}).wait_send()

    @pl.when(returns)
    def _():
        remote(c1r, c1r, snd.at[6], one.at[0], {"dp": dp_c}).wait_send()
        ref = c1r.at[pl.ds(0, PROXIED)]
        remote(ref, ref, snd.at[10], one.at[0], proxy).wait_send()
        many = ipb.at[pl.ds(0, nz - PROXIED), pl.ds(0, cap), pl.ds(0, 3 * chunk)]
        remote(many, many, snd.at[7], one.at[0], {"dp": y_up}).wait_send()
        sent_pieces(nz - PROXIED, snd.at[8])
        slots_copy.wait_send()

    @pl.when(jnp.logical_not(returns))
    def _():
        many = ipb.at[pl.ds(0, PROXIED), pl.ds(0, cap), pl.ds(0, 3 * chunk)]
        remote(many, many, snd.at[7], one.at[0], {"dp": y_up}).wait_send()
        swap.wait_send()

    @pl.when(jnp.logical_not(returns) & same)
    def _():
        sent_pieces(PROXIED - 1, snd.at[8])

    @pl.when(jnp.logical_not(returns) & jnp.logical_not(same))
    def _():
        sent_pieces(PROXIED, snd.at[8])


def expert_call(tokens, out_grad, ids_t, probs_t, w_gate, w_up, w_down):
    tok_rows, width = tokens.shape
    experts = lax.axis_size("cp")
    nz, ny = experts // 2, lax.axis_size("dp") // 2
    top = ids_t.shape[0]
    cap = tok_rows * top * CAP_NUM // (CAP_DEN * experts)
    ff = w_gate.shape[0]
    rows = experts * cap
    quarter = width // 4
    pay = 2 * tok_rows + 16
    anyspace = pl.BlockSpec(memory_space=pl.ANY)
    vmem = pl.BlockSpec(memory_space=pltpu.VMEM)
    wshape = pltpu.VMEM((ff, width), BF16)
    dma = pltpu.SemaphoreType.DMA
    return pl.pallas_call(
        functools.partial(expert_kernel, (tok_rows, width, experts, cap, nz, ny)),
        out_shape=(
            pltpu.VMEM((width // (2 * ny), tok_rows), BF16),
            pltpu.VMEM((top, tok_rows), F32),
            wshape, wshape, wshape,
        ),
        in_specs=[anyspace, anyspace, vmem, vmem, anyspace, anyspace, anyspace],
        out_specs=(vmem,) * 5,
        scratch_shapes=[
            pltpu.VMEM((nz, pay, quarter), BF16),
            pltpu.VMEM((nz, 2, cap, quarter), BF16),
            pltpu.VMEM((2, rows, width), BF16),
            pltpu.VMEM((ff, width), BF16),
            pltpu.VMEM((ff, width), BF16),
            pltpu.VMEM((ff, width), BF16),
            pltpu.VMEM((rows, ff), BF16),
            pltpu.VMEM((rows, ff), BF16),
            pltpu.VMEM((rows, ff), BF16),
            pltpu.VMEM((nz, 2 * cap, width), BF16),
            pltpu.VMEM((nz, cap, width), BF16),
            pltpu.VMEM((nz, cap, width // ny), BF16),
            pltpu.VMEM((nz, cap, width // ny), BF16),
            pltpu.VMEM((nz, cap, width // ny), BF16),
            pltpu.VMEM((nz, cap, width // ny), BF16),
            pltpu.VMEM((experts, 8, 128), F32),
            pltpu.VMEM((experts, 8, 128), F32),
            pltpu.VMEM((ny * 2, top, tok_rows), F32),
            pltpu.VMEM((width // (2 * ny), tok_rows), F32),
            pltpu.VMEM((width // (2 * ny), tok_rows), F32),
            pltpu.VMEM((16, tok_rows), BF16),
            dma((5,)), dma((9,)), dma((nz,)), dma((2 * nz,)), dma((2 * nz,)), dma((2 * nz,)),
            dma((2 * nz,)), dma((12,)), dma((nz,)), dma((nz,)), dma((nz,)), dma((nz,)), dma((nz,)),
            dma((PROXIED,)), dma((experts,)), dma((2 * ny,)), dma((2,)), dma((3,)),
        ],
        compiler_params=pltpu.CompilerParams(
            collective_id=0, has_side_effects=True, vmem_limit_bytes=60 * 1024 * 1024
        ),
        name="expert",
    )(tokens, out_grad, ids_t, probs_t, w_gate, w_up, w_down)


def body(tokens, out_grad, probs, expert_ids, w_gate, w_up, w_down):
    passed, prob_grad, gate_grad, up_grad, down_grad = expert_call(
        tokens[0], out_grad[0], expert_ids[0].T, probs[0].T, w_gate[0, 0], w_up[0, 0], w_down[0, 0]
    )
    return (
        passed.T[None],
        prob_grad.T[None],
        gate_grad[None, None],
        up_grad[None, None],
        down_grad[None, None],
    )


def solution(mesh):
    in_specs = (
        P("pp", "cp", None),
        P("pp", "cp", None),
        P("pp", "cp", None),
        P("pp", "cp", None),
        P("pp", "cp", "dp", None),
        P("pp", "cp", "dp", None),
        P("pp", "cp", "dp", None),
    )
    out_specs = (
        P("pp", "cp", "dp"),
        P("pp", "cp", None),
        P("pp", "cp", "dp", None),
        P("pp", "cp", "dp", None),
        P("pp", "cp", "dp", None),
    )
    return jax.shard_map(body, mesh=mesh, in_specs=in_specs, out_specs=out_specs, check_vma=False)
```

```python
import functools
import jax
import jax.numpy as jnp
from jax import lax
from jax.experimental import pallas as pl
from jax.experimental.pallas import tpu as pltpu
from jax.sharding import PartitionSpec as P

CAP_NUM, CAP_DEN = 5, 4
MESH = pl.DeviceIdType.MESH
PROXIED = 3
F32, BF16 = jnp.float32, jnp.bfloat16


def expert_kernel(
    dims, tok, grd, ids, prb, w_gate, w_up, w_down,
    passed_out, prob_out, gg_out, ug_out, dg_out,
    blk, stg, xs, wg, wu, wd, hid, ggp, gup, ipb, c1r, farr, comr, dirr, l3r,
    ptab, pcol, pall, fxs, fxr, tab,
    loc, zr, xr, cr, yt, yg, cf, snd, c1m, fam, com, dim, l3m, pxm, pcm, pam, psn, one,
):
    tok_rows, width, experts, cap, nz, ny = dims
    quarter = width // 4
    route = 16
    pay = 2 * tok_rows + route
    half_pay = tok_rows + route
    dp = lax.axis_index("dp")
    cp = lax.axis_index("cp")
    ndp, ncp = 2 * ny, 2 * nz
    z, xl = cp // 2, cp % 2
    y, core = dp // 2, dp % 2
    half = y % 2
    mine_q = pl.multiple_of((half * 2 + core) * quarter, 128)
    other_q = pl.multiple_of(((1 - half) * 2 + core) * quarter, 128)
    cp_x = z * 2 + (1 - xl)
    dp_c = y * 2 + (1 - core)
    z_up = ((z + 1) % nz) * 2 + xl
    z_dn = ((z + nz - 1) % nz) * 2 + xl
    y_up = ((y + 1) % ny) * 2 + core
    y_dn = ((y + ny - 1) % ny) * 2 + core

    pp = lax.axis_index("pp")
    returns = pp == 1
    same = core == xl
    owner_dp = y * 2 + xl

    def owner(zz):
        return {"cp": zz * 2 + core, "dp": owner_dp}

    def other_owner(zz):
        return {"pp": 1 - pp, "cp": zz * 2 + core, "dp": owner_dp}

    proxy = {"pp": 1 - pp, "cp": cp_x}

    barrier = pltpu.get_barrier_semaphore()

    def greet(where):
        pl.semaphore_signal(barrier, inc=1, device_id=where, device_id_type=MESH)

    for d in range(1, ncp):
        greet({"cp": (cp + d) % ncp})
    for d in range(1, ndp):
        greet({"dp": (dp + d) % ndp})
    greet({"pp": 1 - pp})
    greet(proxy)
    for zz in range(nz):
        greet(other_owner(zz))

    @pl.when(jnp.logical_not(same))
    def _():
        for zz in range(nz):
            greet(owner(zz))

    loads = [
        pltpu.make_async_copy(
            tok.at[:, pl.ds(mine_q, quarter)], blk.at[z, pl.ds(0, tok_rows), :], loc.at[0]
        ),
        pltpu.make_async_copy(
            grd.at[:, pl.ds(mine_q, quarter)], blk.at[z, pl.ds(half_pay, tok_rows), :], loc.at[1]
        ),
    ]
    weights = [
        pltpu.make_async_copy(w_gate, wg, loc.at[2]),
        pltpu.make_async_copy(w_up, wu, loc.at[3]),
        pltpu.make_async_copy(w_down, wd, loc.at[4]),
    ]
    for c in loads:
        c.start()
    for c in weights:
        c.start()

    e_iota = lax.broadcasted_iota(jnp.int32, (experts, tok_rows), 0)
    has = jnp.zeros((experts, tok_rows), F32)
    wgt = jnp.zeros((experts, tok_rows), F32)
    id_val = ids[...]
    prb_val = prb[...].astype(F32)
    for k in range(id_val.shape[0]):
        hit = id_val[k : k + 1, :] == e_iota
        has = jnp.where(hit, 1.0, has)
        wgt = jnp.where(hit, prb_val[k : k + 1, :], wgt)
    earlier = (
        lax.broadcasted_iota(jnp.int32, (tok_rows, tok_rows), 0)
        < lax.broadcasted_iota(jnp.int32, (tok_rows, tok_rows), 1)
    )
    slot = jnp.dot(
        has.astype(BF16), jnp.where(earlier, 1.0, 0.0).astype(BF16), preferred_element_type=F32
    )
    slot = jnp.where(has > 0.0, slot, -1.0)
    blk[z, tok_rows:half_pay, :] = jnp.zeros((route, quarter), BF16)
    blk[z, tok_rows:half_pay, 0:tok_rows] = slot.astype(BF16)
    blk[z, tok_rows:half_pay, tok_rows : 2 * tok_rows] = wgt.astype(BF16)
    for c in loads:
        c.wait()
    ptab[...] = jnp.zeros_like(ptab)
    pl.semaphore_wait(barrier, ncp + ndp + nz + jnp.where(same, 0, nz))

    def remote(src, dst, s, r, where):
        return pltpu.make_async_remote_copy(
            src_ref=src, dst_ref=dst, send_sem=s, recv_sem=r, device_id=where, device_id_type=MESH
        )

    first, second = pl.ds(0, half_pay), pl.ds(half_pay, tok_rows)
    s_z, s_x, s_c, s_t, s_g, s_f = (snd.at[j] for j in range(6))
    slots_copy = remote(
        blk.at[z, pl.ds(tok_rows, route), pl.ds(0, tok_rows)], tab, snd.at[9], one.at[1], {"pp": 0}
    )

    @pl.when(returns)
    def _():
        slots_copy.start()

    def z_at(i):
        away = (i + 1) // 2
        return (z + nz + jnp.where(i % 2 == 1, -away, away)) % nz

    def block_rows(zz, kind):
        lane = jnp.where(kind == 0, xl, 1 - xl)
        return pl.multiple_of((zz * 2 + lane) * cap, 16)

    def x_copy(i):
        zz = z_at(i)
        dst = xs.at[:, pl.ds(pl.multiple_of((zz * 2 + xl) * cap, 16), cap), pl.ds(mine_q, quarter)]
        return remote(stg.at[i], dst, s_x, xr.at[i], {"cp": cp_x})

    def share(i, kind):
        unit = kind * nz + i
        rows = pl.ds(block_rows(z_at(i), kind), cap)
        cols = pl.ds(mine_q, quarter)
        piece = xs.at[:, rows, cols]
        top, low = xs.at[0, rows, cols], xs.at[1, rows, cols]
        return (
            remote(piece, piece, s_c, cr.at[unit], {"dp": dp_c}),
            remote(top, top, s_t, yt.at[unit], {"dp": y_up}),
            remote(low, low, s_g, yg.at[unit], {"dp": y_dn}),
        )

    def from_y(i, kind):
        unit = kind * nz + i
        rows = pl.ds(block_rows(z_at(i), kind), cap)
        cols = pl.ds(other_q, quarter)
        piece = xs.at[:, rows, cols]
        top, low = xs.at[0, rows, cols], xs.at[1, rows, cols]
        return (
            remote(top, top, s_t, yt.at[unit], {"dp": y_up}),
            remote(low, low, s_g, yg.at[unit], {"dp": y_dn}),
            remote(piece, piece, s_f, cf.at[unit], {"dp": dp_c}),
        )

    def forward(i, kind):
        got_t, got_g, fwd = from_y(i, kind)
        got_t.wait_recv()
        got_g.wait_recv()
        fwd.start()

    def stage_block(i):
        zz = z_at(i)
        whole = blk.at[zz]

        @pl.when((i >= 1) & (i <= 6))
        def _():
            remote(whole, whole, s_z, zr.at[i], {"cp": z_up}).wait_recv()

        @pl.when(i == 7)
        def _():
            a, b = blk.at[zz, first, :], blk.at[zz, second, :]
            remote(a, a, s_z, zr.at[7], {"cp": z_up}).wait_recv()
            remote(b, b, s_z, zr.at[8], {"cp": z_dn}).wait_recv()

        @pl.when((i == 0) | (i == 1) | (i == 3))
        def _():
            remote(whole, whole, s_z, zr.at[jnp.where(i == 0, 1, i + 2)], {"cp": z_up}).start()

        @pl.when((i == 0) | (i == 2) | (i == 4))
        def _():
            remote(whole, whole, s_z, zr.at[i + 2], {"cp": z_dn}).start()

        @pl.when(i == 5)
        def _():
            a = blk.at[zz, first, :]
            remote(a, a, s_z, zr.at[7], {"cp": z_up}).start()

        @pl.when(i == 6)
        def _():
            b = blk.at[zz, second, :]
            remote(b, b, s_z, zr.at[8], {"cp": z_dn}).start()

        table = blk[zz, tok_rows:half_pay, 0 : 2 * tok_rows].astype(F32)
        slots, probs = table[:, :tok_rows], table[:, tok_rows:]
        c_iota = lax.broadcasted_iota(jnp.int32, (cap, tok_rows), 0).astype(F32)
        plain, scaled = [], []
        for expert in (cp, cp_x):
            sel = e_iota == expert
            s_row = jnp.sum(jnp.where(sel, slots, 0.0), axis=0, keepdims=True)
            p_row = jnp.sum(jnp.where(sel, probs, 0.0), axis=0, keepdims=True)
            hit = c_iota == s_row
            plain.append(jnp.where(hit, 1.0, 0.0).astype(BF16))
            scaled.append(jnp.where(hit, p_row, 0.0).astype(BF16))
        rows = pl.ds(block_rows(zz, 0), cap)
        cols = pl.ds(mine_q, quarter)
        for part, lo, onehots in ((0, 0, plain), (1, half_pay, scaled)):
            data = blk[zz, lo : lo + tok_rows, :]
            both = jnp.dot(
                jnp.concatenate(onehots, axis=0), data, preferred_element_type=F32
            ).astype(BF16)
            xs[part, rows, cols] = both[:cap]
            stg[i, part] = both[cap:]
        x_copy(i).start()
        for c in share(i, 0):
            c.start()

    by_feature = (((1,), (1,)), ((), ()))
    by_row = (((0,), (0,)), ((), ()))
    pair = 2 * cap

    chunk = width // ny
    half_w = chunk // 2

    def ccols(yy):
        return pl.ds(pl.multiple_of(yy * chunk, 128), chunk)

    def mine_of(i):
        return ipb.at[i, pl.ds(pl.multiple_of(core * cap, 16), cap)]

    def core_sum(i):
        src = ipb.at[i, pl.ds(pl.multiple_of((1 - core) * cap, 16), cap)]
        return remote(src, c1r.at[i], snd.at[6], c1m.at[i], {"dp": dp_c})

    def y_steps(i):
        up = i % 2 == 0
        fwd_y = jnp.where(up, (y + 1) % ny, (y + ny - 1) % ny)
        bwd_y = jnp.where(up, (y + ny - 1) % ny, (y + 1) % ny)
        fwd_to, bwd_to = {"dp": fwd_y * 2 + core}, {"dp": bwd_y * 2 + core}
        rows = pl.ds(pl.multiple_of(core * cap, 16), cap)
        s_y = snd.at[7]
        far = remote(
            ipb.at[i, rows, ccols((y + 2) % ny)], farr.at[i], s_y, fam.at[i], fwd_to
        )
        comb = remote(ipb.at[i, rows, ccols(fwd_y)], comr.at[i], s_y, com.at[i], fwd_to)
        direct = remote(ipb.at[i, rows, ccols(bwd_y)], dirr.at[i], s_y, dim.at[i], bwd_to)
        return far, comb, direct, fwd_y, rows

    def owner_copy(i, where):
        rows = pl.ds(pl.multiple_of(core * cap, 16), cap)
        return remote(ipb.at[i, rows, ccols(y)], l3r.at[z], snd.at[8], l3m.at[z], where)

    def proxy_copy(i):
        return remote(mine_of(i), mine_of(i), snd.at[10], pxm.at[i], proxy)

    def ret_a(i):
        core_sum(i).wait_recv()
        rows = pl.ds(pl.multiple_of(core * cap, 16), cap)
        ipb[i, rows, :] = (ipb[i, rows, :].astype(F32) + c1r[i].astype(F32)).astype(BF16)

        @pl.when(i < PROXIED)
        def _():
            proxy_copy(i).start()

        @pl.when(i >= PROXIED)
        def _():
            far, _, direct, _, _ = y_steps(i)
            far.start()
            direct.start()

    def proxy_a(i):
        proxy_copy(i).wait_recv()
        far, _, direct, _, _ = y_steps(i)
        far.start()
        direct.start()

    def ret_b(i):
        far, comb, _, fwd_y, rows = y_steps(i)
        far.wait_recv()
        cols = ccols(fwd_y)
        ipb[i, rows, cols] = (ipb[i, rows, cols].astype(F32) + farr[i].astype(F32)).astype(BF16)
        comb.start()

    def ret_c(i):
        _, comb, direct, _, rows = y_steps(i)
        comb.wait_recv()
        direct.wait_recv()
        total = ipb[i, rows, ccols(y)].astype(F32) + comr[i].astype(F32) + dirr[i].astype(F32)
        here = same & (i == 0) & jnp.logical_not(returns)

        @pl.when(here)
        def _():
            l3r[z] = total.astype(BF16)

        @pl.when(jnp.logical_not(here))
        def _():
            ipb[i, rows, ccols(y)] = total.astype(BF16)

            @pl.when(returns)
            def _():
                owner_copy(i, {"pp": 0, **owner(z_at(i))}).start()

            @pl.when(jnp.logical_not(returns))
            def _():
                owner_copy(i, owner(z_at(i))).start()

    def prob_send(i, k):
        zz = z_at(i)
        here = (i == 0) & (xl == k)

        @pl.when(here)
        def _():
            pcol[cp] = ptab[cp]

        @pl.when(jnp.logical_not(here))
        def _():
            remote(
                ptab.at[zz * 2 + k], pcol.at[cp], psn.at[0], pcm.at[cp], {"cp": zz * 2 + k}
            ).start()

    def compute(i):
        zz = z_at(i)
        for kind in (0, 1):
            own, _, _ = share(i, kind)
            own.wait_recv()
            _, _, fwd = from_y(i, kind)
            fwd.wait_recv()
        rows = pl.ds(pl.multiple_of(zz * pair, 16), pair)
        x_rows = xs[0, rows, :]
        gate_pre = lax.dot_general(x_rows, wg[...], by_feature, preferred_element_type=F32)
        up_pre = lax.dot_general(x_rows, wu[...], by_feature, preferred_element_type=F32)
        g_hid = lax.dot_general(xs[1, rows, :], wd[...], by_feature, preferred_element_type=F32)
        sigma = jax.nn.sigmoid(gate_pre)
        silu = gate_pre * sigma
        hidden = (silu * up_pre).astype(BF16)
        hid[rows, :] = hidden
        prod = hidden.astype(F32) * g_hid
        high = prod.astype(BF16)
        low = (prod - high.astype(F32)).astype(BF16)
        ones = jnp.ones((8, prod.shape[1]), BF16)
        for k in (0, 1):
            part = slice(k * cap, (k + 1) * cap)
            sums = lax.dot_general(ones, high[part], by_feature, preferred_element_type=F32)
            sums += lax.dot_general(ones, low[part], by_feature, preferred_element_type=F32)
            ptab[zz * 2 + k, :, 0:cap] = sums
            prob_send(i, k)
        g_gate = (g_hid * up_pre * sigma * (1.0 + gate_pre * (1.0 - sigma))).astype(BF16)
        g_up = (g_hid * silu).astype(BF16)
        ggp[rows, :] = g_gate
        gup[rows, :] = g_up

        @pl.when(returns)
        def _():
            step = 512
            for lo in range(0, width, step):
                part = jnp.dot(g_gate, wg[:, lo : lo + step], preferred_element_type=F32)
                part += jnp.dot(g_up, wu[:, lo : lo + step], preferred_element_type=F32)
                ipb[i, :, lo : lo + step] = part.astype(BF16)
            core_sum(i).start()

    def own_hits(table, expert):
        row = jnp.sum(jnp.where(e_iota == expert, table, 0.0), axis=0, keepdims=True)
        c_iota = lax.broadcasted_iota(jnp.int32, (cap, tok_rows), 0).astype(F32)
        return jnp.where(c_iota == row, 1.0, 0.0).astype(BF16)

    def dp_copy(d):
        return remote(
            pall.at[dp], pall.at[dp], psn.at[1], pam.at[dp], {"dp": (dp + d) % ndp}
        )

    def prob_pick():
        for d in range(1, ncp):
            src = (cp + d) % ncp
            remote(
                pcol.at[src], pcol.at[src], psn.at[0], pcm.at[src], {"cp": src}
            ).wait_recv()
        acc = jnp.zeros(id_val.shape, F32)
        table = blk[z, tok_rows:half_pay, 0:tok_rows].astype(F32)
        for expert in range(experts):
            val = pcol[expert][:, 0:cap]
            high = val.astype(BF16)
            low = (val - high.astype(F32)).astype(BF16)
            hits = own_hits(table, expert)
            got = jnp.dot(high, hits, preferred_element_type=F32)
            got += jnp.dot(low, hits, preferred_element_type=F32)
            acc = jnp.where(ids[...] == expert, got, acc)
        pall[dp] = acc
        for d in range(1, ndp):
            dp_copy(d).start()

    def prob_finish():
        total = pall[dp]
        for d in range(1, ndp):
            src = (dp + d) % ndp
            remote(
                pall.at[src], pall.at[src], psn.at[1], pam.at[src], {"dp": src}
            ).wait_recv()
            total += pall[src]
        prob_out[...] = total / prb[...].astype(F32)

    grad_step = 512
    n_grad = width // grad_step

    def grads(t):
        cols = pl.ds(pl.multiple_of(t * grad_step, 128), grad_step)
        x_cols = xs[0, :, cols]
        gg_out[:, cols] = lax.dot_general(
            ggp[...], x_cols, by_row, preferred_element_type=F32
        ).astype(BF16)
        ug_out[:, cols] = lax.dot_general(
            gup[...], x_cols, by_row, preferred_element_type=F32
        ).astype(BF16)
        dg_out[:, cols] = lax.dot_general(
            hid[...], xs[1, :, cols], by_row, preferred_element_type=F32
        ).astype(BF16)

    def step_fn(i, carry):
        @pl.when(i < nz)
        def _():
            stage_block(i)

        @pl.when((i >= 1) & (i < nz + 1))
        def _():
            x_copy(i - 1).wait_recv()
            for c in share(i - 1, 1):
                c.start()

        @pl.when((i >= 2) & (i < nz + 2))
        def _():
            forward(i - 2, 0)

        @pl.when((i >= 3) & (i < nz + 3))
        def _():
            forward(i - 3, 1)

        @pl.when(i == 4)
        def _():
            for c in weights:
                c.wait()

        for lag, low, stage in ((9, PROXIED, ret_c), (7, PROXIED, ret_b), (5, 0, ret_a)):

            @pl.when(returns & (i >= lag + low) & (i < nz + lag))
            def _(lag=lag, stage=stage):
                stage(i - lag)

        for lag, stage in ((14, ret_c), (12, ret_b), (10, proxy_a)):

            @pl.when(jnp.logical_not(returns) & (i >= lag) & (i < 2 * PROXIED + lag) & (i % 2 == 0))
            def _(lag=lag, stage=stage):
                stage((i - lag) // 2)

        @pl.when((i >= 4) & (i < nz + 4))
        def _():
            compute(i - 4)

        first_free = nz + 4

        @pl.when(i == first_free + 4)
        def _():
            prob_pick()

        first_grad = first_free + jnp.where(returns, 5, 0)

        @pl.when((i >= first_grad) & (i < first_grad + n_grad))
        def _():
            grads(i - first_grad)

        return carry

    lax.fori_loop(0, nz + 4 + 5 + n_grad, step_fn, 0)

    swap = remote(fxs, fxr, snd.at[11], one.at[2], {"dp": dp_c})

    @pl.when(returns)
    def _():
        passed_out[...] = jnp.zeros_like(passed_out)

    @pl.when(jnp.logical_not(returns))
    def _():
        slots_copy.wait_recv()
        table = tab[...].astype(F32)
        tot = jnp.zeros((chunk, tok_rows), F32)
        for i in range(nz):
            away = (i + 1) // 2
            src = (z + nz + (away if i % 2 == 1 else -away)) % nz
            landed = remote(l3r.at[src], l3r.at[src], snd.at[8], l3m.at[src], owner(z))
            if i == 0:
                pl.when(jnp.logical_not(same))(landed.wait_recv)
            else:
                landed.wait_recv()
            hits = own_hits(table, src * 2 + (1 - core if i < PROXIED else core))
            tot += lax.dot_general(l3r[src], hits, by_row, preferred_element_type=F32)

        @pl.when(core == 0)
        def _():
            fxs[...] = tot[half_w:]

        @pl.when(core == 1)
        def _():
            fxs[...] = tot[:half_w]

        swap.start()
        kept = jnp.where(core == 0, tot[:half_w], tot[half_w:])
        swap.wait_recv()
        passed_out[...] = (kept + fxr[...]).astype(BF16)

    prob_finish()
    cols, ocols = pl.ds(mine_q, quarter), pl.ds(other_q, quarter)
    seven = blk.at[pl.ds(0, nz - 1)]
    remote(seven, seven, s_z, zr.at[0], {"cp": z_up}).wait_send()
    remote(stg, stg, s_x, zr.at[0], {"cp": cp_x}).wait_send()
    a = xs.at[:, :, cols]
    remote(a, a, s_c, zr.at[0], {"dp": dp_c}).wait_send()
    a = xs.at[0, :, cols]
    remote(a, a, s_t, zr.at[0], {"dp": y_up}).wait_send()
    a = xs.at[1, :, cols]
    remote(a, a, s_g, zr.at[0], {"dp": y_dn}).wait_send()
    a = xs.at[:, :, ocols]
    remote(a, a, s_f, zr.at[0], {"dp": dp_c}).wait_send()
    most = pcol.at[pl.ds(0, experts - 1)]
    remote(most, most, psn.at[0], one.at[0], {"cp": z_up}).wait_send()
    most = pall.at[pl.ds(0, ndp - 1)]
    remote(most, most, psn.at[1], one.at[0], {"dp": y_up}).wait_send()

    def sent_pieces(pieces, sem):
        ref = dirr.at[pl.ds(0, pieces)]
        remote(ref, ref, sem, one.at[0], {"dp": y_up}).wait_send()

    @pl.when(returns)
    def _():
        remote(c1r, c1r, snd.at[6], one.at[0], {"dp": dp_c}).wait_send()
        ref = c1r.at[pl.ds(0, PROXIED)]
        remote(ref, ref, snd.at[10], one.at[0], proxy).wait_send()
        many = ipb.at[pl.ds(0, nz - PROXIED), pl.ds(0, cap), pl.ds(0, 3 * chunk)]
        remote(many, many, snd.at[7], one.at[0], {"dp": y_up}).wait_send()
        sent_pieces(nz - PROXIED, snd.at[8])
        slots_copy.wait_send()

    @pl.when(jnp.logical_not(returns))
    def _():
        many = ipb.at[pl.ds(0, PROXIED), pl.ds(0, cap), pl.ds(0, 3 * chunk)]
        remote(many, many, snd.at[7], one.at[0], {"dp": y_up}).wait_send()
        swap.wait_send()

    @pl.when(jnp.logical_not(returns) & same)
    def _():
        sent_pieces(PROXIED - 1, snd.at[8])

    @pl.when(jnp.logical_not(returns) & jnp.logical_not(same))
    def _():
        sent_pieces(PROXIED, snd.at[8])


def expert_call(tokens, out_grad, ids_t, probs_t, w_gate, w_up, w_down):
    tok_rows, width = tokens.shape
    experts = lax.axis_size("cp")
    nz, ny = experts // 2, lax.axis_size("dp") // 2
    top = ids_t.shape[0]
    cap = tok_rows * top * CAP_NUM // (CAP_DEN * experts)
    ff = w_gate.shape[0]
    rows = experts * cap
    quarter = width // 4
    pay = 2 * tok_rows + 16
    anyspace = pl.BlockSpec(memory_space=pl.ANY)
    vmem = pl.BlockSpec(memory_space=pltpu.VMEM)
    wshape = pltpu.VMEM((ff, width), BF16)
    dma = pltpu.SemaphoreType.DMA
    return pl.pallas_call(
        functools.partial(expert_kernel, (tok_rows, width, experts, cap, nz, ny)),
        out_shape=(
            pltpu.VMEM((width // (2 * ny), tok_rows), BF16),
            pltpu.VMEM((top, tok_rows), F32),
            wshape, wshape, wshape,
        ),
        in_specs=[anyspace, anyspace, vmem, vmem, anyspace, anyspace, anyspace],
        out_specs=(vmem,) * 5,
        scratch_shapes=[
            pltpu.VMEM((nz, pay, quarter), BF16),
            pltpu.VMEM((nz, 2, cap, quarter), BF16),
            pltpu.VMEM((2, rows, width), BF16),
            pltpu.VMEM((ff, width), BF16),
            pltpu.VMEM((ff, width), BF16),
            pltpu.VMEM((ff, width), BF16),
            pltpu.VMEM((rows, ff), BF16),
            pltpu.VMEM((rows, ff), BF16),
            pltpu.VMEM((rows, ff), BF16),
            pltpu.VMEM((nz, 2 * cap, width), BF16),
            pltpu.VMEM((nz, cap, width), BF16),
            pltpu.VMEM((nz, cap, width // ny), BF16),
            pltpu.VMEM((nz, cap, width // ny), BF16),
            pltpu.VMEM((nz, cap, width // ny), BF16),
            pltpu.VMEM((nz, cap, width // ny), BF16),
            pltpu.VMEM((experts, 8, 128), F32),
            pltpu.VMEM((experts, 8, 128), F32),
            pltpu.VMEM((ny * 2, top, tok_rows), F32),
            pltpu.VMEM((width // (2 * ny), tok_rows), F32),
            pltpu.VMEM((width // (2 * ny), tok_rows), F32),
            pltpu.VMEM((16, tok_rows), BF16),
            dma((5,)), dma((9,)), dma((nz,)), dma((2 * nz,)), dma((2 * nz,)), dma((2 * nz,)),
            dma((2 * nz,)), dma((12,)), dma((nz,)), dma((nz,)), dma((nz,)), dma((nz,)), dma((nz,)),
            dma((PROXIED,)), dma((experts,)), dma((2 * ny,)), dma((2,)), dma((3,)),
        ],
        compiler_params=pltpu.CompilerParams(
            collective_id=0, has_side_effects=True, vmem_limit_bytes=60 * 1024 * 1024
        ),
        name="expert",
    )(tokens, out_grad, ids_t, probs_t, w_gate, w_up, w_down)


def body(tokens, out_grad, probs, expert_ids, w_gate, w_up, w_down):
    passed, prob_grad, gate_grad, up_grad, down_grad = expert_call(
        tokens[0], out_grad[0], expert_ids[0].T, probs[0].T, w_gate[0, 0], w_up[0, 0], w_down[0, 0]
    )
    return (
        passed.T[None],
        prob_grad.T[None],
        gate_grad[None, None],
        up_grad[None, None],
        down_grad[None, None],
    )


def solution(mesh):
    in_specs = (
        P("pp", "cp", None),
        P("pp", "cp", None),
        P("pp", "cp", None),
        P("pp", "cp", None),
        P("pp", "cp", "dp", None),
        P("pp", "cp", "dp", None),
        P("pp", "cp", "dp", None),
    )
    out_specs = (
        P("pp", "cp", "dp"),
        P("pp", "cp", None),
        P("pp", "cp", "dp", None),
        P("pp", "cp", "dp", None),
        P("pp", "cp", "dp", None),
    )
    return jax.shard_map(body, mesh=mesh, in_specs=in_specs, out_specs=out_specs, check_vma=False)
```

```python
import functools
import jax
import jax.numpy as jnp
from jax import lax
from jax.experimental import pallas as pl
from jax.experimental.pallas import tpu as pltpu
from jax.sharding import PartitionSpec as P

CAP_NUM, CAP_DEN = 5, 4
MESH = pl.DeviceIdType.MESH
PROXIED = 3
F32, BF16 = jnp.float32, jnp.bfloat16


def expert_kernel(
    dims, tok, grd, ids, prb, w_gate, w_up, w_down,
    passed_out, prob_out, gg_out, ug_out, dg_out,
    blk, stg, xs, wg, wu, wd, hid, ggp, gup, ipb, c1r, farr, comr, dirr, l3r,
    ptab, pcol, pall, fxs, fxr, tab,
    loc, zr, xr, cr, yt, yg, cf, snd, c1m, fam, com, dim, l3m, pxm, pcm, pam, psn, one,
):
    tok_rows, width, experts, cap, nz, ny = dims
    quarter = width // 4
    route = 16
    pay = 2 * tok_rows + route
    half_pay = tok_rows + route
    dp = lax.axis_index("dp")
    cp = lax.axis_index("cp")
    ndp, ncp = 2 * ny, 2 * nz
    z, xl = cp // 2, cp % 2
    y, core = dp // 2, dp % 2
    half = y % 2
    mine_q = pl.multiple_of((half * 2 + core) * quarter, 128)
    other_q = pl.multiple_of(((1 - half) * 2 + core) * quarter, 128)
    cp_x = z * 2 + (1 - xl)
    dp_c = y * 2 + (1 - core)
    z_up = ((z + 1) % nz) * 2 + xl
    z_dn = ((z + nz - 1) % nz) * 2 + xl
    y_up = ((y + 1) % ny) * 2 + core
    y_dn = ((y + ny - 1) % ny) * 2 + core

    pp = lax.axis_index("pp")
    returns = pp == 1
    same = core == xl
    owner_dp = y * 2 + xl

    def owner(zz):
        return {"cp": zz * 2 + core, "dp": owner_dp}

    def other_owner(zz):
        return {"pp": 1 - pp, "cp": zz * 2 + core, "dp": owner_dp}

    proxy = {"pp": 1 - pp, "cp": cp_x}

    barrier = pltpu.get_barrier_semaphore()

    def greet(where):
        pl.semaphore_signal(barrier, inc=1, device_id=where, device_id_type=MESH)

    for d in range(1, ncp):
        greet({"cp": (cp + d) % ncp})
    for d in range(1, ndp):
        greet({"dp": (dp + d) % ndp})
    greet({"pp": 1 - pp})
    greet(proxy)
    for zz in range(nz):
        greet(other_owner(zz))

    @pl.when(jnp.logical_not(same))
    def _():
        for zz in range(nz):
            greet(owner(zz))

    loads = [
        pltpu.make_async_copy(
            tok.at[:, pl.ds(mine_q, quarter)], blk.at[z, pl.ds(0, tok_rows), :], loc.at[0]
        ),
        pltpu.make_async_copy(
            grd.at[:, pl.ds(mine_q, quarter)], blk.at[z, pl.ds(half_pay, tok_rows), :], loc.at[1]
        ),
    ]
    weights = [
        pltpu.make_async_copy(w_gate, wg, loc.at[2]),
        pltpu.make_async_copy(w_up, wu, loc.at[3]),
        pltpu.make_async_copy(w_down, wd, loc.at[4]),
    ]
    for c in loads:
        c.start()
    for c in weights:
        c.start()

    e_iota = lax.broadcasted_iota(jnp.int32, (experts, tok_rows), 0)
    has = jnp.zeros((experts, tok_rows), F32)
    wgt = jnp.zeros((experts, tok_rows), F32)
    id_val = ids[...]
    prb_val = prb[...].astype(F32)
    for k in range(id_val.shape[0]):
        hit = id_val[k : k + 1, :] == e_iota
        has = jnp.where(hit, 1.0, has)
        wgt = jnp.where(hit, prb_val[k : k + 1, :], wgt)
    earlier = (
        lax.broadcasted_iota(jnp.int32, (tok_rows, tok_rows), 0)
        < lax.broadcasted_iota(jnp.int32, (tok_rows, tok_rows), 1)
    )
    slot = jnp.dot(
        has.astype(BF16), jnp.where(earlier, 1.0, 0.0).astype(BF16), preferred_element_type=F32
    )
    slot = jnp.where(has > 0.0, slot, -1.0)
    blk[z, tok_rows:half_pay, :] = jnp.zeros((route, quarter), BF16)
    blk[z, tok_rows:half_pay, 0:tok_rows] = slot.astype(BF16)
    blk[z, tok_rows:half_pay, tok_rows : 2 * tok_rows] = wgt.astype(BF16)
    for c in loads:
        c.wait()
    ptab[...] = jnp.zeros_like(ptab)
    pl.semaphore_wait(barrier, ncp + ndp + nz + jnp.where(same, 0, nz))

    def remote(src, dst, s, r, where):
        return pltpu.make_async_remote_copy(
            src_ref=src, dst_ref=dst, send_sem=s, recv_sem=r, device_id=where, device_id_type=MESH
        )

    first, second = pl.ds(0, half_pay), pl.ds(half_pay, tok_rows)
    s_z, s_x, s_c, s_t, s_g, s_f = (snd.at[j] for j in range(6))
    slots_copy = remote(
        blk.at[z, pl.ds(tok_rows, route), pl.ds(0, tok_rows)], tab, snd.at[9], one.at[1], {"pp": 0}
    )

    @pl.when(returns)
    def _():
        slots_copy.start()

    def z_at(i):
        away = (i + 1) // 2
        return (z + nz + jnp.where(i % 2 == 1, -away, away)) % nz

    def block_rows(zz, kind):
        lane = jnp.where(kind == 0, xl, 1 - xl)
        return pl.multiple_of((zz * 2 + lane) * cap, 16)

    def x_copy(i):
        zz = z_at(i)
        dst = xs.at[:, pl.ds(pl.multiple_of((zz * 2 + xl) * cap, 16), cap), pl.ds(mine_q, quarter)]
        return remote(stg.at[i], dst, s_x, xr.at[i], {"cp": cp_x})

    def share(i, kind):
        unit = kind * nz + i
        rows = pl.ds(block_rows(z_at(i), kind), cap)
        cols = pl.ds(mine_q, quarter)
        piece = xs.at[:, rows, cols]
        top, low = xs.at[0, rows, cols], xs.at[1, rows, cols]
        return (
            remote(piece, piece, s_c, cr.at[unit], {"dp": dp_c}),
            remote(top, top, s_t, yt.at[unit], {"dp": y_up}),
            remote(low, low, s_g, yg.at[unit], {"dp": y_dn}),
        )

    def from_y(i, kind):
        unit = kind * nz + i
        rows = pl.ds(block_rows(z_at(i), kind), cap)
        cols = pl.ds(other_q, quarter)
        piece = xs.at[:, rows, cols]
        top, low = xs.at[0, rows, cols], xs.at[1, rows, cols]
        return (
            remote(top, top, s_t, yt.at[unit], {"dp": y_up}),
            remote(low, low, s_g, yg.at[unit], {"dp": y_dn}),
            remote(piece, piece, s_f, cf.at[unit], {"dp": dp_c}),
        )

    def forward(i, kind):
        got_t, got_g, fwd = from_y(i, kind)
        got_t.wait_recv()
        got_g.wait_recv()
        fwd.start()

    def stage_block(i):
        zz = z_at(i)
        whole = blk.at[zz]

        @pl.when((i >= 1) & (i <= 6))
        def _():
            remote(whole, whole, s_z, zr.at[i], {"cp": z_up}).wait_recv()

        @pl.when(i == 7)
        def _():
            a, b = blk.at[zz, first, :], blk.at[zz, second, :]
            remote(a, a, s_z, zr.at[7], {"cp": z_up}).wait_recv()
            remote(b, b, s_z, zr.at[8], {"cp": z_dn}).wait_recv()

        @pl.when((i == 0) | (i == 1) | (i == 3))
        def _():
            remote(whole, whole, s_z, zr.at[jnp.where(i == 0, 1, i + 2)], {"cp": z_up}).start()

        @pl.when((i == 0) | (i == 2) | (i == 4))
        def _():
            remote(whole, whole, s_z, zr.at[i + 2], {"cp": z_dn}).start()

        @pl.when(i == 5)
        def _():
            a = blk.at[zz, first, :]
            remote(a, a, s_z, zr.at[7], {"cp": z_up}).start()

        @pl.when(i == 6)
        def _():
            b = blk.at[zz, second, :]
            remote(b, b, s_z, zr.at[8], {"cp": z_dn}).start()

        table = blk[zz, tok_rows:half_pay, 0 : 2 * tok_rows].astype(F32)
        slots, probs = table[:, :tok_rows], table[:, tok_rows:]
        c_iota = lax.broadcasted_iota(jnp.int32, (cap, tok_rows), 0).astype(F32)
        plain, scaled = [], []
        for expert in (cp, cp_x):
            sel = e_iota == expert
            s_row = jnp.sum(jnp.where(sel, slots, 0.0), axis=0, keepdims=True)
            p_row = jnp.sum(jnp.where(sel, probs, 0.0), axis=0, keepdims=True)
            hit = c_iota == s_row
            plain.append(jnp.where(hit, 1.0, 0.0).astype(BF16))
            scaled.append(jnp.where(hit, p_row, 0.0).astype(BF16))
        rows = pl.ds(block_rows(zz, 0), cap)
        cols = pl.ds(mine_q, quarter)
        for part, lo, onehots in ((0, 0, plain), (1, half_pay, scaled)):
            data = blk[zz, lo : lo + tok_rows, :]
            both = jnp.dot(
                jnp.concatenate(onehots, axis=0), data, preferred_element_type=F32
            ).astype(BF16)
            xs[part, rows, cols] = both[:cap]
            stg[i, part] = both[cap:]
        x_copy(i).start()
        for c in share(i, 0):
            c.start()

    by_feature = (((1,), (1,)), ((), ()))
    by_row = (((0,), (0,)), ((), ()))
    pair = 2 * cap

    chunk = width // ny
    half_w = chunk // 2

    def ccols(yy):
        return pl.ds(pl.multiple_of(yy * chunk, 128), chunk)

    def mine_of(i):
        return ipb.at[i, pl.ds(pl.multiple_of(core * cap, 16), cap)]

    def core_sum(i):
        src = ipb.at[i, pl.ds(pl.multiple_of((1 - core) * cap, 16), cap)]
        return remote(src, c1r.at[i], snd.at[6], c1m.at[i], {"dp": dp_c})

    def y_steps(i):
        up = i % 2 == 0
        fwd_y = jnp.where(up, (y + 1) % ny, (y + ny - 1) % ny)
        bwd_y = jnp.where(up, (y + ny - 1) % ny, (y + 1) % ny)
        fwd_to, bwd_to = {"dp": fwd_y * 2 + core}, {"dp": bwd_y * 2 + core}
        rows = pl.ds(pl.multiple_of(core * cap, 16), cap)
        s_y = snd.at[7]
        far = remote(
            ipb.at[i, rows, ccols((y + 2) % ny)], farr.at[i], s_y, fam.at[i], fwd_to
        )
        comb = remote(ipb.at[i, rows, ccols(fwd_y)], comr.at[i], s_y, com.at[i], fwd_to)
        direct = remote(ipb.at[i, rows, ccols(bwd_y)], dirr.at[i], s_y, dim.at[i], bwd_to)
        return far, comb, direct, fwd_y, rows

    def owner_copy(i, where):
        rows = pl.ds(pl.multiple_of(core * cap, 16), cap)
        return remote(ipb.at[i, rows, ccols(y)], l3r.at[z], snd.at[8], l3m.at[z], where)

    def proxy_copy(i):
        return remote(mine_of(i), mine_of(i), snd.at[10], pxm.at[i], proxy)

    def ret_a(i):
        core_sum(i).wait_recv()
        rows = pl.ds(pl.multiple_of(core * cap, 16), cap)
        ipb[i, rows, :] = (ipb[i, rows, :].astype(F32) + c1r[i].astype(F32)).astype(BF16)

        @pl.when(i < PROXIED)
        def _():
            proxy_copy(i).start()

        @pl.when(i >= PROXIED)
        def _():
            far, _, direct, _, _ = y_steps(i)
            far.start()
            direct.start()

    def proxy_a(i):
        proxy_copy(i).wait_recv()
        far, _, direct, _, _ = y_steps(i)
        far.start()
        direct.start()

    def ret_b(i):
        far, comb, _, fwd_y, rows = y_steps(i)
        far.wait_recv()
        cols = ccols(fwd_y)
        ipb[i, rows, cols] = (ipb[i, rows, cols].astype(F32) + farr[i].astype(F32)).astype(BF16)
        comb.start()

    def ret_c(i):
        _, comb, direct, _, rows = y_steps(i)
        comb.wait_recv()
        direct.wait_recv()
        total = ipb[i, rows, ccols(y)].astype(F32) + comr[i].astype(F32) + dirr[i].astype(F32)
        here = same & (i == 0) & jnp.logical_not(returns)

        @pl.when(here)
        def _():
            l3r[z] = total.astype(BF16)

        @pl.when(jnp.logical_not(here))
        def _():
            ipb[i, rows, ccols(y)] = total.astype(BF16)

            @pl.when(returns)
            def _():
                owner_copy(i, {"pp": 0, **owner(z_at(i))}).start()

            @pl.when(jnp.logical_not(returns))
            def _():
                owner_copy(i, owner(z_at(i))).start()

    def prob_send(i, k):
        zz = z_at(i)
        here = (i == 0) & (xl == k)

        @pl.when(here)
        def _():
            pcol[cp] = ptab[cp]

        @pl.when(jnp.logical_not(here))
        def _():
            remote(
                ptab.at[zz * 2 + k], pcol.at[cp], psn.at[0], pcm.at[cp], {"cp": zz * 2 + k}
            ).start()

    def compute(i):
        zz = z_at(i)
        for kind in (0, 1):
            own, _, _ = share(i, kind)
            own.wait_recv()
            _, _, fwd = from_y(i, kind)
            fwd.wait_recv()
        rows = pl.ds(pl.multiple_of(zz * pair, 16), pair)
        x_rows = xs[0, rows, :]
        gate_pre = lax.dot_general(x_rows, wg[...], by_feature, preferred_element_type=F32)
        up_pre = lax.dot_general(x_rows, wu[...], by_feature, preferred_element_type=F32)
        g_hid = lax.dot_general(xs[1, rows, :], wd[...], by_feature, preferred_element_type=F32)
        sigma = jax.nn.sigmoid(gate_pre)
        silu = gate_pre * sigma
        hidden = (silu * up_pre).astype(BF16)
        hid[rows, :] = hidden
        prod = hidden.astype(F32) * g_hid
        high = prod.astype(BF16)
        low = (prod - high.astype(F32)).astype(BF16)
        ones = jnp.ones((8, prod.shape[1]), BF16)
        for k in (0, 1):
            part = slice(k * cap, (k + 1) * cap)
            sums = lax.dot_general(ones, high[part], by_feature, preferred_element_type=F32)
            sums += lax.dot_general(ones, low[part], by_feature, preferred_element_type=F32)
            ptab[zz * 2 + k, :, 0:cap] = sums
            prob_send(i, k)
        g_gate = (g_hid * up_pre * sigma * (1.0 + gate_pre * (1.0 - sigma))).astype(BF16)
        g_up = (g_hid * silu).astype(BF16)
        ggp[rows, :] = g_gate
        gup[rows, :] = g_up

        @pl.when(returns)
        def _():
            step = 512
            for lo in range(0, width, step):
                part = jnp.dot(g_gate, wg[:, lo : lo + step], preferred_element_type=F32)
                part += jnp.dot(g_up, wu[:, lo : lo + step], preferred_element_type=F32)
                ipb[i, :, lo : lo + step] = part.astype(BF16)
            core_sum(i).start()

    def own_hits(table, expert):
        row = jnp.sum(jnp.where(e_iota == expert, table, 0.0), axis=0, keepdims=True)
        c_iota = lax.broadcasted_iota(jnp.int32, (cap, tok_rows), 0).astype(F32)
        return jnp.where(c_iota == row, 1.0, 0.0).astype(BF16)

    def dp_copy(d):
        return remote(
            pall.at[dp], pall.at[dp], psn.at[1], pam.at[dp], {"dp": (dp + d) % ndp}
        )

    def prob_pick():
        for d in range(1, ncp):
            src = (cp + d) % ncp
            remote(
                pcol.at[src], pcol.at[src], psn.at[0], pcm.at[src], {"cp": src}
            ).wait_recv()
        acc = jnp.zeros(id_val.shape, F32)
        table = blk[z, tok_rows:half_pay, 0:tok_rows].astype(F32)
        for expert in range(experts):
            val = pcol[expert][:, 0:cap]
            high = val.astype(BF16)
            low = (val - high.astype(F32)).astype(BF16)
            hits = own_hits(table, expert)
            got = jnp.dot(high, hits, preferred_element_type=F32)
            got += jnp.dot(low, hits, preferred_element_type=F32)
            acc = jnp.where(ids[...] == expert, got, acc)
        pall[dp] = acc
        for d in range(1, ndp):
            dp_copy(d).start()

    def prob_finish():
        total = pall[dp]
        for d in range(1, ndp):
            src = (dp + d) % ndp
            remote(
                pall.at[src], pall.at[src], psn.at[1], pam.at[src], {"dp": src}
            ).wait_recv()
            total += pall[src]
        prob_out[...] = total / prb[...].astype(F32)

    grad_step = 512
    n_grad = width // grad_step

    def grads(t):
        cols = pl.ds(pl.multiple_of(t * grad_step, 128), grad_step)
        x_cols = xs[0, :, cols]
        gg_out[:, cols] = lax.dot_general(
            ggp[...], x_cols, by_row, preferred_element_type=F32
        ).astype(BF16)
        ug_out[:, cols] = lax.dot_general(
            gup[...], x_cols, by_row, preferred_element_type=F32
        ).astype(BF16)
        dg_out[:, cols] = lax.dot_general(
            hid[...], xs[1, :, cols], by_row, preferred_element_type=F32
        ).astype(BF16)

    def step_fn(i, carry):
        @pl.when(returns & (i >= 5) & (i < nz + 5))
        def _():
            ret_a(i - 5)

        @pl.when(i < nz)
        def _():
            stage_block(i)

        @pl.when((i >= 1) & (i < nz + 1))
        def _():
            x_copy(i - 1).wait_recv()
            for c in share(i - 1, 1):
                c.start()

        @pl.when((i >= 2) & (i < nz + 2))
        def _():
            forward(i - 2, 0)

        @pl.when((i >= 3) & (i < nz + 3))
        def _():
            forward(i - 3, 1)

        @pl.when(i == 4)
        def _():
            for c in weights:
                c.wait()

        for lag, low, stage in ((9, PROXIED, ret_c), (7, PROXIED, ret_b)):

            @pl.when(returns & (i >= lag + low) & (i < nz + lag))
            def _(lag=lag, stage=stage):
                stage(i - lag)

        for lag, stage in ((14, ret_c), (12, ret_b), (10, proxy_a)):

            @pl.when(jnp.logical_not(returns) & (i >= lag) & (i < 2 * PROXIED + lag) & (i % 2 == 0))
            def _(lag=lag, stage=stage):
                stage((i - lag) // 2)

        @pl.when((i >= 4) & (i < nz + 4))
        def _():
            compute(i - 4)

        first_free = nz + 4

        @pl.when(i == first_free + 4)
        def _():
            prob_pick()

        first_grad = first_free + jnp.where(returns, 5, 0)

        @pl.when((i >= first_grad) & (i < first_grad + n_grad))
        def _():
            grads(i - first_grad)

        return carry

    lax.fori_loop(0, nz + 4 + 5 + n_grad, step_fn, 0)

    swap = remote(fxs, fxr, snd.at[11], one.at[2], {"dp": dp_c})

    @pl.when(returns)
    def _():
        passed_out[...] = jnp.zeros_like(passed_out)

    @pl.when(jnp.logical_not(returns))
    def _():
        slots_copy.wait_recv()
        table = tab[...].astype(F32)
        tot = jnp.zeros((chunk, tok_rows), F32)
        for i in range(nz):
            away = (i + 1) // 2
            src = (z + nz + (away if i % 2 == 1 else -away)) % nz
            landed = remote(l3r.at[src], l3r.at[src], snd.at[8], l3m.at[src], owner(z))
            if i == 0:
                pl.when(jnp.logical_not(same))(landed.wait_recv)
            else:
                landed.wait_recv()
            hits = own_hits(table, src * 2 + (1 - core if i < PROXIED else core))
            tot += lax.dot_general(l3r[src], hits, by_row, preferred_element_type=F32)

        @pl.when(core == 0)
        def _():
            fxs[...] = tot[half_w:]

        @pl.when(core == 1)
        def _():
            fxs[...] = tot[:half_w]

        swap.start()
        kept = jnp.where(core == 0, tot[:half_w], tot[half_w:])
        swap.wait_recv()
        passed_out[...] = (kept + fxr[...]).astype(BF16)

    prob_finish()
    cols, ocols = pl.ds(mine_q, quarter), pl.ds(other_q, quarter)
    seven = blk.at[pl.ds(0, nz - 1)]
    remote(seven, seven, s_z, zr.at[0], {"cp": z_up}).wait_send()
    remote(stg, stg, s_x, zr.at[0], {"cp": cp_x}).wait_send()
    a = xs.at[:, :, cols]
    remote(a, a, s_c, zr.at[0], {"dp": dp_c}).wait_send()
    a = xs.at[0, :, cols]
    remote(a, a, s_t, zr.at[0], {"dp": y_up}).wait_send()
    a = xs.at[1, :, cols]
    remote(a, a, s_g, zr.at[0], {"dp": y_dn}).wait_send()
    a = xs.at[:, :, ocols]
    remote(a, a, s_f, zr.at[0], {"dp": dp_c}).wait_send()
    most = pcol.at[pl.ds(0, experts - 1)]
    remote(most, most, psn.at[0], one.at[0], {"cp": z_up}).wait_send()
    most = pall.at[pl.ds(0, ndp - 1)]
    remote(most, most, psn.at[1], one.at[0], {"dp": y_up}).wait_send()

    def sent_pieces(pieces, sem):
        ref = dirr.at[pl.ds(0, pieces)]
        remote(ref, ref, sem, one.at[0], {"dp": y_up}).wait_send()

    @pl.when(returns)
    def _():
        remote(c1r, c1r, snd.at[6], one.at[0], {"dp": dp_c}).wait_send()
        ref = c1r.at[pl.ds(0, PROXIED)]
        remote(ref, ref, snd.at[10], one.at[0], proxy).wait_send()
        many = ipb.at[pl.ds(0, nz - PROXIED), pl.ds(0, cap), pl.ds(0, 3 * chunk)]
        remote(many, many, snd.at[7], one.at[0], {"dp": y_up}).wait_send()
        sent_pieces(nz - PROXIED, snd.at[8])
        slots_copy.wait_send()

    @pl.when(jnp.logical_not(returns))
    def _():
        many = ipb.at[pl.ds(0, PROXIED), pl.ds(0, cap), pl.ds(0, 3 * chunk)]
        remote(many, many, snd.at[7], one.at[0], {"dp": y_up}).wait_send()
        swap.wait_send()

    @pl.when(jnp.logical_not(returns) & same)
    def _():
        sent_pieces(PROXIED - 1, snd.at[8])

    @pl.when(jnp.logical_not(returns) & jnp.logical_not(same))
    def _():
        sent_pieces(PROXIED, snd.at[8])


def expert_call(tokens, out_grad, ids_t, probs_t, w_gate, w_up, w_down):
    tok_rows, width = tokens.shape
    experts = lax.axis_size("cp")
    nz, ny = experts // 2, lax.axis_size("dp") // 2
    top = ids_t.shape[0]
    cap = tok_rows * top * CAP_NUM // (CAP_DEN * experts)
    ff = w_gate.shape[0]
    rows = experts * cap
    quarter = width // 4
    pay = 2 * tok_rows + 16
    anyspace = pl.BlockSpec(memory_space=pl.ANY)
    vmem = pl.BlockSpec(memory_space=pltpu.VMEM)
    wshape = pltpu.VMEM((ff, width), BF16)
    dma = pltpu.SemaphoreType.DMA
    return pl.pallas_call(
        functools.partial(expert_kernel, (tok_rows, width, experts, cap, nz, ny)),
        out_shape=(
            pltpu.VMEM((width // (2 * ny), tok_rows), BF16),
            pltpu.VMEM((top, tok_rows), F32),
            wshape, wshape, wshape,
        ),
        in_specs=[anyspace, anyspace, vmem, vmem, anyspace, anyspace, anyspace],
        out_specs=(vmem,) * 5,
        scratch_shapes=[
            pltpu.VMEM((nz, pay, quarter), BF16),
            pltpu.VMEM((nz, 2, cap, quarter), BF16),
            pltpu.VMEM((2, rows, width), BF16),
            pltpu.VMEM((ff, width), BF16),
            pltpu.VMEM((ff, width), BF16),
            pltpu.VMEM((ff, width), BF16),
            pltpu.VMEM((rows, ff), BF16),
            pltpu.VMEM((rows, ff), BF16),
            pltpu.VMEM((rows, ff), BF16),
            pltpu.VMEM((nz, 2 * cap, width), BF16),
            pltpu.VMEM((nz, cap, width), BF16),
            pltpu.VMEM((nz, cap, width // ny), BF16),
            pltpu.VMEM((nz, cap, width // ny), BF16),
            pltpu.VMEM((nz, cap, width // ny), BF16),
            pltpu.VMEM((nz, cap, width // ny), BF16),
            pltpu.VMEM((experts, 8, 128), F32),
            pltpu.VMEM((experts, 8, 128), F32),
            pltpu.VMEM((ny * 2, top, tok_rows), F32),
            pltpu.VMEM((width // (2 * ny), tok_rows), F32),
            pltpu.VMEM((width // (2 * ny), tok_rows), F32),
            pltpu.VMEM((16, tok_rows), BF16),
            dma((5,)), dma((9,)), dma((nz,)), dma((2 * nz,)), dma((2 * nz,)), dma((2 * nz,)),
            dma((2 * nz,)), dma((12,)), dma((nz,)), dma((nz,)), dma((nz,)), dma((nz,)), dma((nz,)),
            dma((PROXIED,)), dma((experts,)), dma((2 * ny,)), dma((2,)), dma((3,)),
        ],
        compiler_params=pltpu.CompilerParams(
            collective_id=0, has_side_effects=True, vmem_limit_bytes=60 * 1024 * 1024
        ),
        name="expert",
    )(tokens, out_grad, ids_t, probs_t, w_gate, w_up, w_down)


def body(tokens, out_grad, probs, expert_ids, w_gate, w_up, w_down):
    passed, prob_grad, gate_grad, up_grad, down_grad = expert_call(
        tokens[0], out_grad[0], expert_ids[0].T, probs[0].T, w_gate[0, 0], w_up[0, 0], w_down[0, 0]
    )
    return (
        passed.T[None],
        prob_grad.T[None],
        gate_grad[None, None],
        up_grad[None, None],
        down_grad[None, None],
    )


def solution(mesh):
    in_specs = (
        P("pp", "cp", None),
        P("pp", "cp", None),
        P("pp", "cp", None),
        P("pp", "cp", None),
        P("pp", "cp", "dp", None),
        P("pp", "cp", "dp", None),
        P("pp", "cp", "dp", None),
    )
    out_specs = (
        P("pp", "cp", "dp"),
        P("pp", "cp", None),
        P("pp", "cp", "dp", None),
        P("pp", "cp", "dp", None),
        P("pp", "cp", "dp", None),
    )
    return jax.shard_map(body, mesh=mesh, in_specs=in_specs, out_specs=out_specs, check_vma=False)
```
